32 devices in a mesh: seq: 8 (over z, core), head: 4 (over y, x).
Axes of the slice: x: 2, y: 2, z: 4, core: 2. Of those that a mesh axis runs over, the one named last changes fastest.
Arguments:
- inputs: float32 [8192, 5120], P(('seq', 'head')), may hold values from -6 to 6
- log_decay: float32 [8192, 80], P(('seq', 'head')), may hold values from -1 to 0
- input_map: float32 [8192, 128], P(('seq', 'head')), may hold values from -0.31533617 to 0.31533617
- output_map: float32 [8192, 128], P(('seq', 'head')), may hold values from -0.31533617 to 0.31533617
- skip_gain: float32 [80], replicated, may hold values from 0.5 to 2
Outputs:
- outputs: float32 [8192, 5120], P(('seq', 'head'))
The draws below stay inside these ranges and needn't reach their ends.
All inputs are finite; a program needn't handle non-finite values.
Results may differ from the reference program's by a relative error of at most 0.0001.
Values sent between devices are 32-bit elements; how exact they have to be, the bound alone decides.
A program may use at most 128 MiB of HBM per device.

```python
import math
from functools import partial
import jax
import jax.numpy as jnp
from jax import lax

HEADS = 80
HEAD_DIM = 64
STATE = 128
BLOCK = 128
TOK_DEV = 256
TOKEN_TOTAL = 8192


def draw_log_decay(key, part):
    fast_share = 0.2
    middle_share = 0.3
    class_key = jax.random.fold_in(key, 11)
    fast_rate_key = jax.random.fold_in(key, 12)
    slow_rate_key = jax.random.fold_in(key, 13)
    block_key = jax.random.fold_in(key, 14)
    jitter_key = jax.random.fold_in(key, 15)
    spike_random_key = jax.random.fold_in(key, 16)
    height_random_key = jax.random.fold_in(key, 17)
    middle_rate_key = jax.random.fold_in(key, 18)
    pick = jax.random.uniform(class_key, (HEADS,), jnp.float32)
    is_fast = pick < fast_share
    is_middle = jnp.logical_and(pick >= fast_share, pick < fast_share + middle_share)
    fast_rates = jnp.exp(jax.random.uniform(fast_rate_key, (HEADS,), jnp.float32, math.log(1.0 / 50.0), math.log(1.0 / 30.0)))
    middle_rates = jnp.exp(jax.random.uniform(middle_rate_key, (HEADS,), jnp.float32, math.log(0.0001), math.log(0.003)))
    slow_rates = jnp.exp(jax.random.uniform(slow_rate_key, (HEADS,), jnp.float32, math.log(0.05), math.log(0.35))) / TOKEN_TOTAL
    rates = jnp.where(is_fast, fast_rates, jnp.where(is_middle, middle_rates, slow_rates))
    block_scale = jnp.exp(jax.random.uniform(block_key, (TOKEN_TOTAL // TOK_DEV,), jnp.float32, math.log(0.6), math.log(1.6)))
    block_scale = jnp.repeat(block_scale, TOK_DEV)[:, None]
    jitter = jax.random.uniform(jitter_key, (TOKEN_TOTAL, HEADS), jnp.float32, 0.7, 1.3)
    value_entries = -rates[None, :] * block_scale * jitter
    spike_positions = jax.random.randint(spike_random_key, (2,), 0, TOKEN_TOTAL)
    spike_height = jnp.log(jax.random.uniform(height_random_key, (2,), jnp.float32, 0.5, 0.8))
    spike_hits = (jnp.arange(TOKEN_TOTAL)[:, None] == spike_positions[None, :]).astype(jnp.float32)
    value_entries = value_entries + jnp.sum(spike_hits * spike_height[None, :], axis=1)[:, None]
    return value_entries.astype(jnp.float32)


def level_of(own_key, dims, cuts, smallest, top_value):
    gain = 1.0
    for axis_at, parts in cuts:
        draws = jax.random.uniform(jax.random.fold_in(jax.random.fold_in(own_key, 6), axis_at), (parts,), jnp.float32, smallest / len(cuts), top_value / len(cuts))
        gain = gain * jnp.repeat(jnp.exp(draws), dims[axis_at] // parts).reshape((-1,) + (1,) * (len(dims) - 1 - axis_at))
    return gain


def gaussian(stream_key, dims, scale, limit, cuts=(), held_as=jnp.bfloat16):
    array = jax.random.normal(stream_key, dims, jnp.float32) * scale
    if len(cuts) > 0:
        array = level_of(stream_key, dims, cuts, -0.22, 0.18) * array
    return jnp.clip(array, min=-limit, max=limit).astype(held_as)


def setup_inputs(seed: int = 0) -> dict:
    keys = jax.random.split(jax.random.key(seed), 6)
    return {
        "inputs": gaussian(keys[0], (TOKEN_TOTAL, HEADS * HEAD_DIM), 1.0, 6.0, ((0, 32),), jnp.float32),
        "log_decay": draw_log_decay(jax.random.fold_in(keys[5], 71), 0),
        "input_map": gaussian(keys[2], (TOKEN_TOTAL, STATE), ((STATE * 1024) ** -0.25), 0.31533617, ((0, 32),), jnp.float32),
        "output_map": gaussian(keys[3], (TOKEN_TOTAL, STATE), ((STATE * 1024) ** -0.25), 0.31533617, ((0, 32),), jnp.float32),
        "skip_gain": jnp.clip(jnp.exp(jax.random.uniform(keys[4], (HEADS,), jnp.float32, math.log(0.5), math.log(2.0))), 0.5, 2.0),
    }


PRECISE = lax.Precision.HIGHEST


def block_pass(loop_carry, pieces, head_dim):
    memory, summed = loop_carry
    x_block, d_block, b_block, c_block = pieces
    length = d_block.shape[0]
    head_count = d_block.shape[1]
    running = jnp.cumsum(d_block, axis=0)
    positions = jnp.arange(length)
    causal = positions[:, None] >= positions[None, :]
    spread = running.T[:, :, None] - running.T[:, None, :]
    decays = jnp.where(causal[None], jnp.exp(jnp.minimum(spread, 0.0)), 0.0)
    scores = jnp.dot(c_block, b_block.T, precision=PRECISE)
    weighted = scores[None] * decays
    per_head = x_block.reshape(length, head_count, head_dim)
    within = jnp.einsum("hij,jhp->ihp", weighted, per_head, precision=PRECISE).reshape(length, head_count * head_dim)
    growth = jnp.repeat(jnp.exp(running), head_dim, axis=1)
    carried = jnp.dot(c_block, memory, precision=PRECISE) * growth
    closing = running[-1]
    remains = jnp.repeat(jnp.exp(closing[None, :] - running), head_dim, axis=1)
    memory = jnp.repeat(jnp.exp(closing), head_dim)[None, :] * memory + jnp.dot(b_block.T, x_block * remains, precision=PRECISE)
    prefix = running + summed[None, :]
    return (memory, summed + closing), (within + carried, prefix)


def scan_blocks(inputs, log_decay, input_map, output_map, memory, head_dim):
    token_count = inputs.shape[0]
    blocks = token_count // BLOCK
    pieces = (inputs.reshape(blocks, BLOCK, -1), log_decay.reshape(blocks, BLOCK, -1),
              input_map.reshape(blocks, BLOCK, -1), output_map.reshape(blocks, BLOCK, -1))
    start = jnp.zeros((log_decay.shape[1],), jnp.float32)
    (memory, summed), (results, prefix) = lax.scan(partial(block_pass, head_dim=head_dim), (memory, start), pieces)
    return results.reshape(token_count, -1), prefix.reshape(token_count, -1), memory, summed


def reference(inputs, log_decay, input_map, output_map, skip_gain):
    memory = jnp.zeros((STATE, HEADS * HEAD_DIM), jnp.float32)
    results, prefix, memory, summed = scan_blocks(inputs, log_decay, input_map, output_map, memory, HEAD_DIM)
    return results + inputs * jnp.repeat(skip_gain, HEAD_DIM)[None, :]
```

```python
import functools
import jax
import jax.numpy as jnp
from jax import lax
from jax.experimental import pallas as pl
from jax.experimental.pallas import tpu as pltpu
from jax.sharding import PartitionSpec as P

BLOCK = 128


PRECISE = lax.Precision.HIGHEST


def from_behind(value, axis, steps):
    count = lax.axis_size(axis)
    leading, last = (max(0, -steps), min(count, count - steps))
    return lax.ppermute(value, axis, [(source, source + steps) for source in range(leading, last)])


def scan_blocks(inputs, log_decay, input_map, output_map, head_dim):
    token_count = inputs.shape[0]
    width = inputs.shape[1]
    head_count = log_decay.shape[1]
    state_width = input_map.shape[1]
    blocks = token_count // BLOCK
    x_all = inputs.reshape(blocks, BLOCK, width)
    d_all = log_decay.reshape(blocks, BLOCK, head_count)
    b_all = input_map.reshape(blocks, BLOCK, state_width)
    c_all = output_map.reshape(blocks, BLOCK, state_width)
    running = jnp.cumsum(d_all, axis=1)
    run_heads = jnp.moveaxis(running, 2, 1)
    positions = jnp.arange(BLOCK)
    causal = positions[:, None] >= positions[None, :]
    spread = run_heads[:, :, :, None] - run_heads[:, :, None, :]
    decays = jnp.where(causal[None, None], jnp.exp(jnp.minimum(spread, 0.0)), 0.0)
    scores = jnp.einsum("bin,bjn->bij", c_all, b_all, precision=PRECISE)
    weighted = scores[:, None] * decays
    per_head = x_all.reshape(blocks, BLOCK, head_count, head_dim)
    within = jnp.einsum("bhij,bjhp->bihp", weighted, per_head, precision=PRECISE).reshape(
        blocks, BLOCK, width
    )
    closing = running[:, -1, :]
    remains = jnp.repeat(jnp.exp(closing[:, None, :] - running), head_dim, axis=2)
    own_state = jnp.einsum("bln,blw->bnw", b_all, x_all * remains, precision=PRECISE)
    totals = jnp.cumsum(closing, axis=0)
    before_total = totals - closing
    order = jnp.arange(blocks)
    earlier = order[:, None] > order[None, :]
    gap = before_total[:, None, :] - totals[None, :, :]
    link = jnp.where(earlier[:, :, None], jnp.exp(jnp.minimum(gap, 0.0)), 0.0)
    link_wide = jnp.repeat(link, head_dim, axis=2)
    entering = jnp.einsum("kjw,jnw->knw", link_wide, own_state, precision=PRECISE)
    final_weight = jnp.repeat(jnp.exp(totals[-1][None, :] - totals), head_dim, axis=1)
    memory = jnp.einsum("jw,jnw->nw", final_weight, own_state, precision=PRECISE)
    growth = jnp.repeat(jnp.exp(running), head_dim, axis=2)
    carried = jnp.einsum("bin,bnw->biw", c_all, entering, precision=PRECISE) * growth
    prefix = running + before_total[:, None, :]
    return (
        (within + carried).reshape(token_count, width),
        prefix.reshape(token_count, head_count),
        memory,
        totals[-1],
    )


def shard_chain(summed, memory, head_dim):
    factor = jnp.repeat(jnp.exp(summed), head_dim)[None, :]

    def advance(turn, incoming):
        return from_behind(factor * incoming + memory, "seq", 1)

    return lax.fori_loop(0, lax.axis_size("seq") - 1, advance, jnp.zeros_like(memory))


def on_device(inputs, log_decay, input_map, output_map, skip_gain):
    head_count = skip_gain.shape[0]
    head_dim = inputs.shape[1] // head_count
    state_width = input_map.shape[1]
    groups = lax.axis_size("head")
    local_heads = head_count // groups
    local_width = local_heads * head_dim
    results, prefix, memory, summed = scan_blocks(
        inputs, log_decay, input_map, output_map, head_dim
    )
    got_sum, got_state = (
        lax.all_to_all(
            summed.reshape(1, groups, local_heads), "head", split_axis=1, concat_axis=1, tiled=True
        ),
        lax.all_to_all(
            memory.reshape(state_width, groups, local_width),
            "head",
            split_axis=1,
            concat_axis=1,
            tiled=True,
        ),
    )

    def within_shard(carry, item):
        total_decay, total_state = carry
        decay_here, state_here = item
        scale_now = jnp.repeat(jnp.exp(decay_here), head_dim)[None, :]
        return ((total_decay + decay_here, scale_now * total_state + state_here), carry)

    start_carry = (
        jnp.zeros((local_heads,), jnp.float32),
        jnp.zeros((state_width, local_width), jnp.float32),
    )
    (shard_decay, shard_state), (before_decay, before_state) = lax.scan(
        within_shard, start_carry, (got_sum[0], jnp.moveaxis(got_state, 1, 0))
    )
    incoming = shard_chain(shard_decay, shard_state, head_dim)
    per_source = (
        jnp.repeat(jnp.exp(before_decay), head_dim, axis=1)[:, None, :] * incoming[None]
        + before_state
    )
    back = lax.all_to_all(
        jnp.moveaxis(per_source, 0, 1), "head", split_axis=1, concat_axis=1, tiled=True
    )
    arrived = back.reshape(state_width, head_count * head_dim)
    returned = results + jnp.dot(output_map, arrived, precision=PRECISE) * jnp.repeat(
        jnp.exp(prefix), head_dim, axis=1
    )
    return returned + inputs * jnp.repeat(skip_gain, head_dim)[None, :]


MESH = pl.DeviceIdType.MESH
CHUNK = 256
LANES = 128


def two(value):
    high = value.astype(jnp.bfloat16)
    return high, (value - high.astype(jnp.float32)).astype(jnp.bfloat16)


def three(value):
    high = value.astype(jnp.bfloat16)
    rest = value - high.astype(jnp.float32)
    middle = rest.astype(jnp.bfloat16)
    return high, middle, (rest - middle.astype(jnp.float32)).astype(jnp.bfloat16)


def left_side(value):
    high, low = two(value)
    return jnp.concatenate([high, high, low], axis=1)


def right_side(value):
    high, low = two(value)
    return jnp.concatenate([high, low, high], axis=0)


def mm(a, b):
    return jnp.dot(a, b, preferred_element_type=jnp.float32)


def full_mm(a, b, dims):
    return lax.dot_general(
        a, b, (dims, ((), ())), precision=PRECISE, preferred_element_type=jnp.float32
    )


def expander(chunk, depth, heads_per_chunk, head_dim):
    row = lax.broadcasted_iota(jnp.int32, (depth, CHUNK), 0) & (LANES - 1)
    column = lax.broadcasted_iota(jnp.int32, (depth, CHUNK), 1) // head_dim
    hit = row == column + chunk * heads_per_chunk
    return jnp.where(hit, 1.0, 0.0).astype(jnp.bfloat16)


def whole_kernel(
    groups, shards, head_dim,
    x_hbm, d_ref, b_ref, c_ref, g_ref, o_hbm,
    xbuf, obuf, mbuf, rbuf, sbuf, sout, back,
    first, second, readout, spread, grow, rows,
    xsem, osem, fsend, frecv, csend, crecv, bsend, brecv,
):
    seq = lax.axis_index("seq")
    me = lax.axis_index("head")
    chunks = xbuf.shape[0]
    per = chunks // groups
    state = b_ref.shape[1]
    hpc = CHUNK // head_dim

    def x_copy(chunk):
        columns = pl.ds(pl.multiple_of(chunk * CHUNK, CHUNK), CHUNK)
        return pltpu.make_async_copy(x_hbm.at[:, columns], xbuf.at[chunk], xsem.at[chunk])

    def o_copy(chunk):
        columns = pl.ds(pl.multiple_of(chunk * CHUNK, CHUNK), CHUNK)
        return pltpu.make_async_copy(obuf.at[chunk], o_hbm.at[:, columns], osem.at[chunk])

    def at_turn(turn):
        k = turn // groups
        owner = (me + 1 + turn % groups) % groups
        return k, owner, owner * per + k

    def forth(chunk, k, owner):
        return pltpu.make_async_remote_copy(
            src_ref=mbuf.at[chunk],
            dst_ref=rbuf.at[me * per + k],
            send_sem=fsend.at[chunk],
            recv_sem=frecv.at[me * per + k],
            device_id={"head": owner},
            device_id_type=MESH,
        )

    def forth_in(slot):
        return pltpu.make_async_remote_copy(
            src_ref=mbuf.at[slot],
            dst_ref=rbuf.at[slot],
            send_sem=fsend.at[slot],
            recv_sem=frecv.at[slot],
            device_id={"head": (me + 1) % groups},
            device_id_type=MESH,
        )

    def chain(k):
        return pltpu.make_async_remote_copy(
            src_ref=sout.at[k],
            dst_ref=sbuf.at[k],
            send_sem=csend.at[k],
            recv_sem=crecv.at[k],
            device_id={"seq": (seq + 1) % shards},
            device_id_type=MESH,
        )

    def home(slot, k, target):
        return pltpu.make_async_remote_copy(
            src_ref=rbuf.at[slot, pl.ds(0, state)],
            dst_ref=back.at[me * per + k],
            send_sem=bsend.at[slot],
            recv_sem=brecv.at[me * per + k],
            device_id={"head": target},
            device_id_type=MESH,
        )

    def home_in(slot):
        return pltpu.make_async_remote_copy(
            src_ref=rbuf.at[slot, pl.ds(0, state)],
            dst_ref=back.at[slot],
            send_sem=bsend.at[slot],
            recv_sem=brecv.at[slot],
            device_id={"head": (me + 1) % groups},
            device_id_type=MESH,
        )

    def load(turn, carry):
        x_copy(at_turn(turn)[2]).start()
        return carry

    lax.fori_loop(0, chunks, load, 0)

    barrier = pltpu.get_barrier_semaphore()
    for step in range(1, groups):
        pl.semaphore_signal(
            barrier, inc=1, device_id={"head": (me + step) % groups}, device_id_type=MESH
        )
    for step in (1, shards - 1):
        pl.semaphore_signal(
            barrier, inc=1, device_id={"seq": (seq + step) % shards}, device_id_type=MESH
        )

    heads = d_ref.shape[1]
    below = lax.broadcasted_iota(jnp.int32, (BLOCK, BLOCK), 0)
    above = lax.broadcasted_iota(jnp.int32, (BLOCK, BLOCK), 1)
    causal = below >= above
    ones = jnp.where(causal, 1.0, 0.0).astype(jnp.bfloat16)
    padding = jnp.zeros((d_ref.shape[0], LANES - heads), jnp.float32)
    decay = jnp.concatenate([d_ref[...], padding], axis=1)
    run1 = sum(mm(ones, part) for part in three(decay[:BLOCK]))
    run2 = sum(mm(ones, part) for part in three(decay[BLOCK:]))
    end1, end2 = run1[BLOCK - 1 :], run2[BLOCK - 1 :]
    mid1, mid2 = run1[BLOCK // 2 - 1 : BLOCK // 2], run2[BLOCK // 2 - 1 : BLOCK // 2]
    total = end1 + end2
    tables = jnp.concatenate(
        [
            jnp.exp(mid1 - run1),
            jnp.exp(mid2 - run2),
            jnp.exp(run1 - mid1),
            jnp.exp(run2 - mid2),
            jnp.exp(run2 + (end1 - mid1)),
        ],
        axis=0,
    )
    spread[...] = jnp.concatenate(two(tables), axis=1)
    grow[...] = jnp.concatenate(
        two(jnp.concatenate([jnp.exp(run1), jnp.exp(run2 + end1)], axis=0)), axis=1
    )
    gain = jnp.concatenate([g_ref[...], jnp.zeros((1, LANES - heads), jnp.float32)], axis=1)
    line = lax.broadcasted_iota(jnp.int32, (16, LANES), 0)
    picked = jnp.where(line == 0, jnp.exp(total), 0.0)
    picked = jnp.where(line == 1, jnp.exp(total - mid1), picked)
    picked = jnp.where(line == 2, jnp.exp(end2 - mid2), picked)
    picked = jnp.where(line == 3, gain, picked)
    rows[...] = jnp.concatenate(three(picked), axis=1)

    b1, b2 = b_ref[:BLOCK], b_ref[BLOCK:]
    c1, c2 = c_ref[:BLOCK], c_ref[BLOCK:]
    last = ((1,), (1,))
    own1 = jnp.where(causal, full_mm(c1, b1, last), 0.0)
    own2 = jnp.where(causal, full_mm(c2, b2, last), 0.0)
    cross = full_mm(c2, b1, last)
    first[...] = left_side(jnp.concatenate([own1, cross, b1.T], axis=0))
    second[...] = left_side(jnp.concatenate([own2, b2.T], axis=0))
    readout[...] = left_side(c_ref[...])

    @pl.when(seq == 0)
    def _():
        sbuf[...] = jnp.zeros_like(sbuf)

    pl.semaphore_wait(barrier, groups + 1)

    def local(turn, carry):
        k, owner, chunk = at_turn(turn)
        x_copy(chunk).wait()
        x = xbuf[chunk]
        scale = mm(spread[...], expander(chunk, 2 * LANES, hpc, head_dim))
        lines = mm(rows[...], expander(chunk, 3 * LANES, hpc, head_dim))
        weighed = x * scale[: 2 * BLOCK]
        y1 = mm(first[...], right_side(weighed[:BLOCK]))
        y2 = mm(second[...], right_side(weighed[BLOCK:]))
        obuf[chunk, :BLOCK] = y1[:BLOCK] * scale[2 * BLOCK : 3 * BLOCK] + lines[3:4] * x[:BLOCK]
        obuf[chunk, BLOCK:] = (
            y2[:BLOCK] * scale[3 * BLOCK : 4 * BLOCK]
            + y1[BLOCK : 2 * BLOCK] * scale[4 * BLOCK :]
            + lines[3:4] * x[BLOCK:]
        )
        memory = y1[2 * BLOCK :] * lines[1:2] + y2[BLOCK:] * lines[2:3]
        factor = jnp.broadcast_to(lines[0:1], (8, CHUNK))

        @pl.when(owner == me)
        def _():
            rbuf[chunk, :state] = memory
            rbuf[chunk, state:] = factor

        @pl.when(owner != me)
        def _():
            mbuf[chunk, :state] = memory
            mbuf[chunk, state:] = factor
            forth(chunk, k, owner).start()

        return carry

    lax.fori_loop(0, chunks, local, 0)

    def link(k, carry):
        for step in range(1, groups):
            forth_in(((me + step) % groups) * per + k).wait_recv()
        factors = [rbuf[j * per + k, state : state + 1] for j in range(groups)]
        shard = rbuf[k, :state]
        shard_factor = factors[0]
        for j in range(1, groups):
            shard = factors[j] * shard + rbuf[j * per + k, :state]
            shard_factor = shard_factor * factors[j]
        sout[k] = shard

        @pl.when(seq > 0)
        def _():
            chain(k).wait_recv()

        @pl.when(seq < shards - 1)
        def _():
            sout[k] = shard_factor * sbuf[k] + sout[k]
            chain(k).start()

        incoming = sbuf[k]
        for j in range(groups):
            slot = j * per + k
            here = rbuf[slot, :state]
            rbuf[slot, :state] = incoming

            @pl.when(me == j)
            def _():
                back[slot] = incoming

            @pl.when(me != j)
            def _():
                home(slot, k, j).start()

            incoming = factors[j] * incoming + here
        return carry

    lax.fori_loop(0, per, link, 0)

    def finish(turn, carry):
        k = turn // groups
        owner = (me + turn % groups) % groups
        chunk = owner * per + k

        @pl.when(owner != me)
        def _():
            home_in(chunk).wait_recv()

        carried = mm(readout[...], right_side(back[chunk]))
        growth = mm(grow[...], expander(chunk, 2 * LANES, hpc, head_dim))
        obuf[chunk] = obuf[chunk] + carried * growth
        o_copy(chunk).start()
        return carry

    lax.fori_loop(0, chunks, finish, 0)

    def drain(chunk, carry):
        o_copy(chunk).wait()

        @pl.when(chunk // per != me)
        def _():
            forth_in(chunk).wait_send()
            home_in(chunk).wait_send()

        return carry

    lax.fori_loop(0, chunks, drain, 0)

    @pl.when(seq < shards - 1)
    def _():
        def drain_chain(k, carry):
            chain(k).wait_send()
            return carry

        lax.fori_loop(0, per, drain_chain, 0)


def in_one(groups, shards, inputs, log_decay, input_map, output_map, skip_gain):
    tokens, width = inputs.shape
    state = input_map.shape[1]
    chunks = width // CHUNK
    per = chunks // groups
    head_dim = width // skip_gain.shape[0]
    vmem = pl.BlockSpec(memory_space=pltpu.VMEM)
    anywhere = pl.BlockSpec(memory_space=pl.ANY)
    f32, bf16 = jnp.float32, jnp.bfloat16
    dma = pltpu.SemaphoreType.DMA
    return pl.pallas_call(
        functools.partial(whole_kernel, groups, shards, head_dim),
        out_shape=jax.ShapeDtypeStruct((tokens, width), f32),
        in_specs=[anywhere, vmem, vmem, vmem, vmem],
        out_specs=anywhere,
        scratch_shapes=[
            pltpu.VMEM((chunks, tokens, CHUNK), f32),
            pltpu.VMEM((chunks, tokens, CHUNK), f32),
            pltpu.VMEM((chunks, state + 8, CHUNK), f32),
            pltpu.VMEM((chunks, state + 8, CHUNK), f32),
            pltpu.VMEM((per, state, CHUNK), f32),
            pltpu.VMEM((per, state, CHUNK), f32),
            pltpu.VMEM((chunks, state, CHUNK), f32),
            pltpu.VMEM((2 * BLOCK + state, 3 * BLOCK), bf16),
            pltpu.VMEM((BLOCK + state, 3 * BLOCK), bf16),
            pltpu.VMEM((tokens, 3 * state), bf16),
            pltpu.VMEM((5 * BLOCK, 2 * LANES), bf16),
            pltpu.VMEM((2 * BLOCK, 2 * LANES), bf16),
            pltpu.VMEM((16, 3 * LANES), bf16),
            dma((chunks,)),
            dma((chunks,)),
            dma((chunks,)),
            dma((chunks,)),
            dma((per,)),
            dma((per,)),
            dma((chunks,)),
            dma((chunks,)),
        ],
        compiler_params=pltpu.CompilerParams(
            collective_id=0, has_side_effects=True, vmem_limit_bytes=56 << 20
        ),
    )(inputs, log_decay, input_map, output_map, skip_gain.reshape(1, -1))


def on_any(groups, shards, inputs, log_decay, input_map, output_map, skip_gain):
    tokens, width = inputs.shape
    heads = skip_gain.shape[0]
    head_dim = width // heads
    fits = (
        tokens == 2 * BLOCK
        and input_map.shape[1] == LANES
        and heads <= LANES
        and CHUNK % head_dim == 0
        and width % (groups * CHUNK) == 0
        and groups > 1
        and shards > 2
    )
    if fits:
        return in_one(groups, shards, inputs, log_decay, input_map, output_map, skip_gain)
    return on_device(inputs, log_decay, input_map, output_map, skip_gain)


def solution(mesh):
    in_specs = (
        P(("seq", "head"), None),
        P(("seq", "head"), None),
        P(("seq", "head"), None),
        P(("seq", "head"), None),
        P(),
    )
    out_specs = P(("seq", "head"), None)
    return jax.shard_map(
        functools.partial(on_any, mesh.shape["head"], mesh.shape["seq"]),
        mesh=mesh, in_specs=in_specs, out_specs=out_specs, check_vma=False,
    )
```

```python
import functools
import jax
import jax.numpy as jnp
from jax import lax
from jax.experimental import pallas as pl
from jax.experimental.pallas import tpu as pltpu
from jax.sharding import PartitionSpec as P

BLOCK = 128


PRECISE = lax.Precision.HIGHEST


def from_behind(value, axis, steps):
    count = lax.axis_size(axis)
    leading, last = (max(0, -steps), min(count, count - steps))
    return lax.ppermute(value, axis, [(source, source + steps) for source in range(leading, last)])


def scan_blocks(inputs, log_decay, input_map, output_map, head_dim):
    token_count = inputs.shape[0]
    width = inputs.shape[1]
    head_count = log_decay.shape[1]
    state_width = input_map.shape[1]
    blocks = token_count // BLOCK
    x_all = inputs.reshape(blocks, BLOCK, width)
    d_all = log_decay.reshape(blocks, BLOCK, head_count)
    b_all = input_map.reshape(blocks, BLOCK, state_width)
    c_all = output_map.reshape(blocks, BLOCK, state_width)
    running = jnp.cumsum(d_all, axis=1)
    run_heads = jnp.moveaxis(running, 2, 1)
    positions = jnp.arange(BLOCK)
    causal = positions[:, None] >= positions[None, :]
    spread = run_heads[:, :, :, None] - run_heads[:, :, None, :]
    decays = jnp.where(causal[None, None], jnp.exp(jnp.minimum(spread, 0.0)), 0.0)
    scores = jnp.einsum("bin,bjn->bij", c_all, b_all, precision=PRECISE)
    weighted = scores[:, None] * decays
    per_head = x_all.reshape(blocks, BLOCK, head_count, head_dim)
    within = jnp.einsum("bhij,bjhp->bihp", weighted, per_head, precision=PRECISE).reshape(
        blocks, BLOCK, width
    )
    closing = running[:, -1, :]
    remains = jnp.repeat(jnp.exp(closing[:, None, :] - running), head_dim, axis=2)
    own_state = jnp.einsum("bln,blw->bnw", b_all, x_all * remains, precision=PRECISE)
    totals = jnp.cumsum(closing, axis=0)
    before_total = totals - closing
    order = jnp.arange(blocks)
    earlier = order[:, None] > order[None, :]
    gap = before_total[:, None, :] - totals[None, :, :]
    link = jnp.where(earlier[:, :, None], jnp.exp(jnp.minimum(gap, 0.0)), 0.0)
    link_wide = jnp.repeat(link, head_dim, axis=2)
    entering = jnp.einsum("kjw,jnw->knw", link_wide, own_state, precision=PRECISE)
    final_weight = jnp.repeat(jnp.exp(totals[-1][None, :] - totals), head_dim, axis=1)
    memory = jnp.einsum("jw,jnw->nw", final_weight, own_state, precision=PRECISE)
    growth = jnp.repeat(jnp.exp(running), head_dim, axis=2)
    carried = jnp.einsum("bin,bnw->biw", c_all, entering, precision=PRECISE) * growth
    prefix = running + before_total[:, None, :]
    return (
        (within + carried).reshape(token_count, width),
        prefix.reshape(token_count, head_count),
        memory,
        totals[-1],
    )


def shard_chain(summed, memory, head_dim):
    factor = jnp.repeat(jnp.exp(summed), head_dim)[None, :]

    def advance(turn, incoming):
        return from_behind(factor * incoming + memory, "seq", 1)

    return lax.fori_loop(0, lax.axis_size("seq") - 1, advance, jnp.zeros_like(memory))


def on_device(inputs, log_decay, input_map, output_map, skip_gain):
    head_count = skip_gain.shape[0]
    head_dim = inputs.shape[1] // head_count
    state_width = input_map.shape[1]
    groups = lax.axis_size("head")
    local_heads = head_count // groups
    local_width = local_heads * head_dim
    results, prefix, memory, summed = scan_blocks(
        inputs, log_decay, input_map, output_map, head_dim
    )
    got_sum, got_state = (
        lax.all_to_all(
            summed.reshape(1, groups, local_heads), "head", split_axis=1, concat_axis=1, tiled=True
        ),
        lax.all_to_all(
            memory.reshape(state_width, groups, local_width),
            "head",
            split_axis=1,
            concat_axis=1,
            tiled=True,
        ),
    )

    def within_shard(carry, item):
        total_decay, total_state = carry
        decay_here, state_here = item
        scale_now = jnp.repeat(jnp.exp(decay_here), head_dim)[None, :]
        return ((total_decay + decay_here, scale_now * total_state + state_here), carry)

    start_carry = (
        jnp.zeros((local_heads,), jnp.float32),
        jnp.zeros((state_width, local_width), jnp.float32),
    )
    (shard_decay, shard_state), (before_decay, before_state) = lax.scan(
        within_shard, start_carry, (got_sum[0], jnp.moveaxis(got_state, 1, 0))
    )
    incoming = shard_chain(shard_decay, shard_state, head_dim)
    per_source = (
        jnp.repeat(jnp.exp(before_decay), head_dim, axis=1)[:, None, :] * incoming[None]
        + before_state
    )
    back = lax.all_to_all(
        jnp.moveaxis(per_source, 0, 1), "head", split_axis=1, concat_axis=1, tiled=True
    )
    arrived = back.reshape(state_width, head_count * head_dim)
    returned = results + jnp.dot(output_map, arrived, precision=PRECISE) * jnp.repeat(
        jnp.exp(prefix), head_dim, axis=1
    )
    return returned + inputs * jnp.repeat(skip_gain, head_dim)[None, :]


MESH = pl.DeviceIdType.MESH
CHUNK = 256
LANES = 128


def two(value):
    high = value.astype(jnp.bfloat16)
    return high, (value - high.astype(jnp.float32)).astype(jnp.bfloat16)


def three(value):
    high = value.astype(jnp.bfloat16)
    rest = value - high.astype(jnp.float32)
    middle = rest.astype(jnp.bfloat16)
    return high, middle, (rest - middle.astype(jnp.float32)).astype(jnp.bfloat16)


def left_side(value):
    high, low = two(value)
    return jnp.concatenate([high, high, low], axis=1)


def right_side(value):
    high, low = two(value)
    return jnp.concatenate([high, low, high], axis=0)


def mm(a, b):
    return jnp.dot(a, b, preferred_element_type=jnp.float32)


def full_mm(a, b, dims):
    return lax.dot_general(
        a, b, (dims, ((), ())), precision=PRECISE, preferred_element_type=jnp.float32
    )


def expander(chunk, depth, heads_per_chunk, head_dim):
    row = lax.broadcasted_iota(jnp.int32, (depth, CHUNK), 0) & (LANES - 1)
    column = lax.broadcasted_iota(jnp.int32, (depth, CHUNK), 1) // head_dim
    hit = row == column + chunk * heads_per_chunk
    return jnp.where(hit, 1.0, 0.0).astype(jnp.bfloat16)


def whole_kernel(
    groups, shards, head_dim,
    x_hbm, d_ref, b_ref, c_ref, g_ref, o_ref,
    xbuf, mbuf, rbuf, sbuf, sout, back,
    first, second, readout, spread, grow, rows, loss,
    xsem, fsend, frecv, csend, crecv, bsend, brecv, lsend, lrecv,
):
    seq = lax.axis_index("seq")
    me = lax.axis_index("head")
    chunks = xbuf.shape[0]
    per = chunks // groups
    state = b_ref.shape[1]
    hpc = CHUNK // head_dim

    def x_copy(chunk):
        columns = pl.ds(pl.multiple_of(chunk * CHUNK, CHUNK), CHUNK)
        return pltpu.make_async_copy(x_hbm.at[:, columns], xbuf.at[chunk], xsem.at[chunk])

    def columns_of(chunk):
        return pl.ds(pl.multiple_of(chunk * CHUNK, CHUNK), CHUNK)

    def share(step):
        return pltpu.make_async_remote_copy(
            src_ref=loss.at[me],
            dst_ref=loss.at[me],
            send_sem=lsend.at[step],
            recv_sem=lrecv.at[me],
            device_id={"head": (me + step) % groups},
            device_id_type=MESH,
        )

    def share_in(source):
        return pltpu.make_async_remote_copy(
            src_ref=loss.at[source],
            dst_ref=loss.at[source],
            send_sem=lsend.at[0],
            recv_sem=lrecv.at[source],
            device_id={"head": (me + 1) % groups},
            device_id_type=MESH,
        )

    def at_turn(turn):
        k = turn // groups
        owner = (me + 1 + turn % groups) % groups
        return k, owner, owner * per + k

    def forth(chunk, k, owner):
        return pltpu.make_async_remote_copy(
            src_ref=mbuf.at[chunk],
            dst_ref=rbuf.at[me * per + k],
            send_sem=fsend.at[chunk],
            recv_sem=frecv.at[me * per + k],
            device_id={"head": owner},
            device_id_type=MESH,
        )

    def forth_in(slot):
        return pltpu.make_async_remote_copy(
            src_ref=mbuf.at[slot],
            dst_ref=rbuf.at[slot],
            send_sem=fsend.at[slot],
            recv_sem=frecv.at[slot],
            device_id={"head": (me + 1) % groups},
            device_id_type=MESH,
        )

    def chain(k):
        return pltpu.make_async_remote_copy(
            src_ref=sout.at[k],
            dst_ref=sbuf.at[k],
            send_sem=csend.at[k],
            recv_sem=crecv.at[k],
            device_id={"seq": (seq + 1) % shards},
            device_id_type=MESH,
        )

    def home(slot, k, target):
        return pltpu.make_async_remote_copy(
            src_ref=rbuf.at[slot],
            dst_ref=back.at[me * per + k],
            send_sem=bsend.at[slot],
            recv_sem=brecv.at[me * per + k],
            device_id={"head": target},
            device_id_type=MESH,
        )

    def home_in(slot):
        return pltpu.make_async_remote_copy(
            src_ref=rbuf.at[slot],
            dst_ref=back.at[slot],
            send_sem=bsend.at[slot],
            recv_sem=brecv.at[slot],
            device_id={"head": (me + 1) % groups},
            device_id_type=MESH,
        )

    def load(turn, carry):
        x_copy(at_turn(turn)[2]).start()
        return carry

    lax.fori_loop(0, chunks, load, 0)

    barrier = pltpu.get_barrier_semaphore()
    for step in range(1, groups):
        pl.semaphore_signal(
            barrier, inc=1, device_id={"head": (me + step) % groups}, device_id_type=MESH
        )
    for step in (1, shards - 1):
        pl.semaphore_signal(
            barrier, inc=1, device_id={"seq": (seq + step) % shards}, device_id_type=MESH
        )

    heads = d_ref.shape[0]
    below = lax.broadcasted_iota(jnp.int32, (BLOCK, BLOCK), 0)
    above = lax.broadcasted_iota(jnp.int32, (BLOCK, BLOCK), 1)
    causal = below >= above
    ones = jnp.where(causal, 1.0, 0.0).astype(jnp.bfloat16)
    padding = jnp.zeros((LANES - heads, d_ref.shape[1]), jnp.float32)
    decay = jnp.concatenate([d_ref[...], padding], axis=0).T
    run1 = sum(mm(ones, part) for part in three(decay[:BLOCK]))
    run2 = sum(mm(ones, part) for part in three(decay[BLOCK:]))
    end1, end2 = run1[BLOCK - 1 :], run2[BLOCK - 1 :]
    mid1, mid2 = run1[BLOCK // 2 - 1 : BLOCK // 2], run2[BLOCK // 2 - 1 : BLOCK // 2]
    total = end1 + end2
    tables = jnp.concatenate(
        [
            jnp.exp(mid1 - run1),
            jnp.exp(mid2 - run2),
            jnp.exp(run1 - mid1),
            jnp.exp(run2 - mid2),
            jnp.exp(run2 + (end1 - mid1)),
        ],
        axis=0,
    )
    spread[...] = jnp.concatenate(two(tables), axis=1)
    grow[...] = jnp.concatenate(
        two(jnp.concatenate([jnp.exp(run1), jnp.exp(run2 + end1)], axis=0)), axis=1
    )
    gain = jnp.concatenate([g_ref[...], jnp.zeros((1, LANES - heads), jnp.float32)], axis=1)
    line = lax.broadcasted_iota(jnp.int32, (16, LANES), 0)
    picked = jnp.where(line == 1, jnp.exp(total - mid1), 0.0)
    picked = jnp.where(line == 2, jnp.exp(end2 - mid2), picked)
    picked = jnp.where(line == 3, gain, picked)
    rows[...] = jnp.concatenate(three(picked), axis=1)
    loss[me] = jnp.broadcast_to(jnp.exp(total), (8, LANES))

    b1, b2 = b_ref[:BLOCK], b_ref[BLOCK:]
    c1, c2 = c_ref[:BLOCK], c_ref[BLOCK:]
    last = ((1,), (1,))
    own1 = jnp.where(causal, full_mm(c1, b1, last), 0.0)
    own2 = jnp.where(causal, full_mm(c2, b2, last), 0.0)
    cross = full_mm(c2, b1, last)
    first[...] = left_side(jnp.concatenate([own1, cross, b1.T], axis=0))
    second[...] = left_side(jnp.concatenate([own2, b2.T], axis=0))
    readout[...] = left_side(c_ref[...])

    @pl.when(seq == 0)
    def _():
        sbuf[...] = jnp.zeros_like(sbuf)

    pl.semaphore_wait(barrier, groups + 1)
    for step in range(1, groups):
        share(step).start()

    def local(turn, carry):
        k, owner, chunk = at_turn(turn)
        x_copy(chunk).wait()
        x = xbuf[chunk]
        scale = mm(spread[...], expander(chunk, 2 * LANES, hpc, head_dim))
        lines = mm(rows[...], expander(chunk, 3 * LANES, hpc, head_dim))
        weighed = x * scale[: 2 * BLOCK]
        y1 = mm(first[...], right_side(weighed[:BLOCK]))
        y2 = mm(second[...], right_side(weighed[BLOCK:]))
        o_ref[:BLOCK, columns_of(chunk)] = y1[:BLOCK] * scale[2 * BLOCK : 3 * BLOCK] + lines[3:4] * x[:BLOCK]
        o_ref[BLOCK:, columns_of(chunk)] = (
            y2[:BLOCK] * scale[3 * BLOCK : 4 * BLOCK]
            + y1[BLOCK : 2 * BLOCK] * scale[4 * BLOCK :]
            + lines[3:4] * x[BLOCK:]
        )
        memory = y1[2 * BLOCK :] * lines[1:2] + y2[BLOCK:] * lines[2:3]

        @pl.when(owner == me)
        def _():
            rbuf[chunk] = memory

        @pl.when(owner != me)
        def _():
            mbuf[chunk] = memory
            forth(chunk, k, owner).start()

        return carry

    lax.fori_loop(0, chunks, local, 0)

    for step in range(1, groups):
        share_in((me + step) % groups).wait_recv()
    tall = -(-groups // 16) * 16
    line = lax.broadcasted_iota(jnp.int32, (tall, LANES), 0)
    losses = jnp.zeros((tall, LANES), jnp.float32)
    for j in range(groups):
        losses = jnp.where(line == j, loss[j, :1], losses)
    losses = jnp.concatenate(three(losses), axis=1)

    def link(k, carry):
        for step in range(1, groups):
            forth_in(((me + step) % groups) * per + k).wait_recv()
        wide = mm(losses, expander(me * per + k, 3 * LANES, hpc, head_dim))
        factors = [wide[j : j + 1] for j in range(groups)]
        shard = rbuf[k]
        shard_factor = factors[0]
        for j in range(1, groups):
            shard = factors[j] * shard + rbuf[j * per + k]
            shard_factor = shard_factor * factors[j]
        sout[k] = shard

        @pl.when(seq > 0)
        def _():
            chain(k).wait_recv()

        @pl.when(seq < shards - 1)
        def _():
            sout[k] = shard_factor * sbuf[k] + sout[k]
            chain(k).start()

        incoming = sbuf[k]
        for j in range(groups):
            slot = j * per + k
            here = rbuf[slot]
            rbuf[slot] = incoming

            @pl.when(me == j)
            def _():
                back[slot] = incoming

            @pl.when(me != j)
            def _():
                home(slot, k, j).start()

            incoming = factors[j] * incoming + here
        return carry

    lax.fori_loop(0, per, link, 0)

    def finish(turn, carry):
        k = turn // groups
        owner = (me + turn % groups) % groups
        chunk = owner * per + k

        @pl.when(owner != me)
        def _():
            home_in(chunk).wait_recv()

        carried = mm(readout[...], right_side(back[chunk]))
        growth = mm(grow[...], expander(chunk, 2 * LANES, hpc, head_dim))
        columns = columns_of(chunk)
        o_ref[:, columns] = o_ref[:, columns] + carried * growth
        return carry

    lax.fori_loop(0, chunks, finish, 0)

    def drain(chunk, carry):
        @pl.when(chunk // per != me)
        def _():
            forth_in(chunk).wait_send()
            home_in(chunk).wait_send()

        return carry

    lax.fori_loop(0, chunks, drain, 0)
    for step in range(1, groups):
        share(step).wait_send()

    @pl.when(seq < shards - 1)
    def _():
        def drain_chain(k, carry):
            chain(k).wait_send()
            return carry

        lax.fori_loop(0, per, drain_chain, 0)


def in_one(groups, shards, inputs, log_decay, input_map, output_map, skip_gain):
    tokens, width = inputs.shape
    state = input_map.shape[1]
    chunks = width // CHUNK
    per = chunks // groups
    head_dim = width // skip_gain.shape[0]
    vmem = pl.BlockSpec(memory_space=pltpu.VMEM)
    far = pl.BlockSpec(memory_space=pltpu.HBM)
    f32, bf16 = jnp.float32, jnp.bfloat16
    dma = pltpu.SemaphoreType.DMA
    return pl.pallas_call(
        functools.partial(whole_kernel, groups, shards, head_dim),
        out_shape=jax.ShapeDtypeStruct((tokens, width), f32),
        in_specs=[far, vmem, vmem, vmem, vmem],
        out_specs=vmem,
        scratch_shapes=[
            pltpu.VMEM((chunks, tokens, CHUNK), f32),
            pltpu.VMEM((chunks, state, CHUNK), f32),
            pltpu.VMEM((chunks, state, CHUNK), f32),
            pltpu.VMEM((per, state, CHUNK), f32),
            pltpu.VMEM((per, state, CHUNK), f32),
            pltpu.VMEM((chunks, state, CHUNK), f32),
            pltpu.VMEM((2 * BLOCK + state, 3 * BLOCK), bf16),
            pltpu.VMEM((BLOCK + state, 3 * BLOCK), bf16),
            pltpu.VMEM((tokens, 3 * state), bf16),
            pltpu.VMEM((5 * BLOCK, 2 * LANES), bf16),
            pltpu.VMEM((2 * BLOCK, 2 * LANES), bf16),
            pltpu.VMEM((16, 3 * LANES), bf16),
            pltpu.VMEM((groups, 8, LANES), f32),
            dma((chunks,)),
            dma((chunks,)),
            dma((chunks,)),
            dma((per,)),
            dma((per,)),
            dma((chunks,)),
            dma((chunks,)),
            dma((groups,)),
            dma((groups,)),
        ],
        compiler_params=pltpu.CompilerParams(
            collective_id=0, has_side_effects=True, vmem_limit_bytes=36 << 20
        ),
    )(inputs, log_decay.T, input_map, output_map, skip_gain.reshape(1, -1))


def on_any(groups, shards, inputs, log_decay, input_map, output_map, skip_gain):
    tokens, width = inputs.shape
    heads = skip_gain.shape[0]
    head_dim = width // heads
    fits = (
        tokens == 2 * BLOCK
        and input_map.shape[1] == LANES
        and heads <= LANES
        and CHUNK % head_dim == 0
        and width % (groups * CHUNK) == 0
        and groups > 1
        and shards > 2
    )
    if fits:
        return in_one(groups, shards, inputs, log_decay, input_map, output_map, skip_gain)
    return on_device(inputs, log_decay, input_map, output_map, skip_gain)


def solution(mesh):
    in_specs = (
        P(("seq", "head"), None),
        P(("seq", "head"), None),
        P(("seq", "head"), None),
        P(("seq", "head"), None),
        P(),
    )
    out_specs = P(("seq", "head"), None)
    return jax.shard_map(
        functools.partial(on_any, mesh.shape["head"], mesh.shape["seq"]),
        mesh=mesh, in_specs=in_specs, out_specs=out_specs, check_vma=False,
    )
```

```python
import functools
import jax
import jax.numpy as jnp
from jax import lax
from jax.experimental import pallas as pl
from jax.experimental.pallas import tpu as pltpu
from jax.sharding import PartitionSpec as P

BLOCK = 128


PRECISE = lax.Precision.HIGHEST


def from_behind(value, axis, steps):
    count = lax.axis_size(axis)
    leading, last = (max(0, -steps), min(count, count - steps))
    return lax.ppermute(value, axis, [(source, source + steps) for source in range(leading, last)])


def scan_blocks(inputs, log_decay, input_map, output_map, head_dim):
    token_count = inputs.shape[0]
    width = inputs.shape[1]
    head_count = log_decay.shape[1]
    state_width = input_map.shape[1]
    blocks = token_count // BLOCK
    x_all = inputs.reshape(blocks, BLOCK, width)
    d_all = log_decay.reshape(blocks, BLOCK, head_count)
    b_all = input_map.reshape(blocks, BLOCK, state_width)
    c_all = output_map.reshape(blocks, BLOCK, state_width)
    running = jnp.cumsum(d_all, axis=1)
    run_heads = jnp.moveaxis(running, 2, 1)
    positions = jnp.arange(BLOCK)
    causal = positions[:, None] >= positions[None, :]
    spread = run_heads[:, :, :, None] - run_heads[:, :, None, :]
    decays = jnp.where(causal[None, None], jnp.exp(jnp.minimum(spread, 0.0)), 0.0)
    scores = jnp.einsum("bin,bjn->bij", c_all, b_all, precision=PRECISE)
    weighted = scores[:, None] * decays
    per_head = x_all.reshape(blocks, BLOCK, head_count, head_dim)
    within = jnp.einsum("bhij,bjhp->bihp", weighted, per_head, precision=PRECISE).reshape(
        blocks, BLOCK, width
    )
    closing = running[:, -1, :]
    remains = jnp.repeat(jnp.exp(closing[:, None, :] - running), head_dim, axis=2)
    own_state = jnp.einsum("bln,blw->bnw", b_all, x_all * remains, precision=PRECISE)
    totals = jnp.cumsum(closing, axis=0)
    before_total = totals - closing
    order = jnp.arange(blocks)
    earlier = order[:, None] > order[None, :]
    gap = before_total[:, None, :] - totals[None, :, :]
    link = jnp.where(earlier[:, :, None], jnp.exp(jnp.minimum(gap, 0.0)), 0.0)
    link_wide = jnp.repeat(link, head_dim, axis=2)
    entering = jnp.einsum("kjw,jnw->knw", link_wide, own_state, precision=PRECISE)
    final_weight = jnp.repeat(jnp.exp(totals[-1][None, :] - totals), head_dim, axis=1)
    memory = jnp.einsum("jw,jnw->nw", final_weight, own_state, precision=PRECISE)
    growth = jnp.repeat(jnp.exp(running), head_dim, axis=2)
    carried = jnp.einsum("bin,bnw->biw", c_all, entering, precision=PRECISE) * growth
    prefix = running + before_total[:, None, :]
    return (
        (within + carried).reshape(token_count, width),
        prefix.reshape(token_count, head_count),
        memory,
        totals[-1],
    )


def shard_chain(summed, memory, head_dim):
    factor = jnp.repeat(jnp.exp(summed), head_dim)[None, :]

    def advance(turn, incoming):
        return from_behind(factor * incoming + memory, "seq", 1)

    return lax.fori_loop(0, lax.axis_size("seq") - 1, advance, jnp.zeros_like(memory))


def on_device(inputs, log_decay, input_map, output_map, skip_gain):
    head_count = skip_gain.shape[0]
    head_dim = inputs.shape[1] // head_count
    state_width = input_map.shape[1]
    groups = lax.axis_size("head")
    local_heads = head_count // groups
    local_width = local_heads * head_dim
    results, prefix, memory, summed = scan_blocks(
        inputs, log_decay, input_map, output_map, head_dim
    )
    got_sum, got_state = (
        lax.all_to_all(
            summed.reshape(1, groups, local_heads), "head", split_axis=1, concat_axis=1, tiled=True
        ),
        lax.all_to_all(
            memory.reshape(state_width, groups, local_width),
            "head",
            split_axis=1,
            concat_axis=1,
            tiled=True,
        ),
    )

    def within_shard(carry, item):
        total_decay, total_state = carry
        decay_here, state_here = item
        scale_now = jnp.repeat(jnp.exp(decay_here), head_dim)[None, :]
        return ((total_decay + decay_here, scale_now * total_state + state_here), carry)

    start_carry = (
        jnp.zeros((local_heads,), jnp.float32),
        jnp.zeros((state_width, local_width), jnp.float32),
    )
    (shard_decay, shard_state), (before_decay, before_state) = lax.scan(
        within_shard, start_carry, (got_sum[0], jnp.moveaxis(got_state, 1, 0))
    )
    incoming = shard_chain(shard_decay, shard_state, head_dim)
    per_source = (
        jnp.repeat(jnp.exp(before_decay), head_dim, axis=1)[:, None, :] * incoming[None]
        + before_state
    )
    back = lax.all_to_all(
        jnp.moveaxis(per_source, 0, 1), "head", split_axis=1, concat_axis=1, tiled=True
    )
    arrived = back.reshape(state_width, head_count * head_dim)
    returned = results + jnp.dot(output_map, arrived, precision=PRECISE) * jnp.repeat(
        jnp.exp(prefix), head_dim, axis=1
    )
    return returned + inputs * jnp.repeat(skip_gain, head_dim)[None, :]


MESH = pl.DeviceIdType.MESH
CHUNK = 256
LANES = 128


def two(value):
    high = value.astype(jnp.bfloat16)
    return high, (value - high.astype(jnp.float32)).astype(jnp.bfloat16)


def three(value):
    high = value.astype(jnp.bfloat16)
    rest = value - high.astype(jnp.float32)
    middle = rest.astype(jnp.bfloat16)
    return high, middle, (rest - middle.astype(jnp.float32)).astype(jnp.bfloat16)


def left_side(value):
    high, low = two(value)
    return jnp.concatenate([high, high, low], axis=1)


def right_side(value):
    high, low = two(value)
    return jnp.concatenate([high, low, high], axis=0)


def mm(a, b):
    return jnp.dot(a, b, preferred_element_type=jnp.float32)


def full_mm(a, b, dims):
    return lax.dot_general(
        a, b, (dims, ((), ())), precision=PRECISE, preferred_element_type=jnp.float32
    )


def expander(chunk, depth, heads_per_chunk, head_dim):
    row = lax.broadcasted_iota(jnp.int32, (depth, CHUNK), 0) & (LANES - 1)
    column = lax.broadcasted_iota(jnp.int32, (depth, CHUNK), 1) // head_dim
    hit = row == column + chunk * heads_per_chunk
    return jnp.where(hit, 1.0, 0.0).astype(jnp.bfloat16)


def whole_kernel(
    groups, shards, head_dim,
    x_hbm, d_ref, b_ref, c_ref, g_ref, o_ref,
    xbuf, mbuf, rbuf, sbuf, sout, back,
    first, second, readout, spread, grow, rows, loss,
    xsem, fsend, frecv, csend, crecv, bsend, brecv, lsend, lrecv,
):
    seq = lax.axis_index("seq")
    me = lax.axis_index("head")
    chunks = xbuf.shape[0]
    per = chunks // groups
    state = b_ref.shape[1]
    hpc = CHUNK // head_dim

    def x_copy(chunk):
        columns = pl.ds(pl.multiple_of(chunk * CHUNK, CHUNK), CHUNK)
        return pltpu.make_async_copy(x_hbm.at[:, columns], xbuf.at[chunk], xsem.at[chunk])

    def columns_of(chunk):
        return pl.ds(pl.multiple_of(chunk * CHUNK, CHUNK), CHUNK)

    def share(step):
        return pltpu.make_async_remote_copy(
            src_ref=loss.at[me],
            dst_ref=loss.at[me],
            send_sem=lsend.at[step],
            recv_sem=lrecv.at[me],
            device_id={"head": (me + step) % groups},
            device_id_type=MESH,
        )

    def share_in(source):
        return pltpu.make_async_remote_copy(
            src_ref=loss.at[source],
            dst_ref=loss.at[source],
            send_sem=lsend.at[0],
            recv_sem=lrecv.at[source],
            device_id={"head": (me + 1) % groups},
            device_id_type=MESH,
        )

    def at_turn(turn):
        k = turn // groups
        owner = (me + 1 + turn % groups) % groups
        return k, owner, owner * per + k

    def forth(chunk, k, owner):
        return pltpu.make_async_remote_copy(
            src_ref=mbuf.at[chunk],
            dst_ref=rbuf.at[me * per + k],
            send_sem=fsend.at[chunk],
            recv_sem=frecv.at[me * per + k],
            device_id={"head": owner},
            device_id_type=MESH,
        )

    def forth_in(slot):
        return pltpu.make_async_remote_copy(
            src_ref=mbuf.at[slot],
            dst_ref=rbuf.at[slot],
            send_sem=fsend.at[slot],
            recv_sem=frecv.at[slot],
            device_id={"head": (me + 1) % groups},
            device_id_type=MESH,
        )

    def chain(k):
        return pltpu.make_async_remote_copy(
            src_ref=sout.at[k],
            dst_ref=sbuf.at[k],
            send_sem=csend.at[k],
            recv_sem=crecv.at[k],
            device_id={"seq": (seq + 1) % shards},
            device_id_type=MESH,
        )

    def home(slot, k, target):
        return pltpu.make_async_remote_copy(
            src_ref=rbuf.at[slot],
            dst_ref=back.at[me * per + k],
            send_sem=bsend.at[slot],
            recv_sem=brecv.at[me * per + k],
            device_id={"head": target},
            device_id_type=MESH,
        )

    def home_in(slot):
        return pltpu.make_async_remote_copy(
            src_ref=rbuf.at[slot],
            dst_ref=back.at[slot],
            send_sem=bsend.at[slot],
            recv_sem=brecv.at[slot],
            device_id={"head": (me + 1) % groups},
            device_id_type=MESH,
        )

    def load(turn, carry):
        x_copy(at_turn(turn)[2]).start()
        return carry

    lax.fori_loop(0, chunks, load, 0)

    barrier = pltpu.get_barrier_semaphore()
    for step in range(1, groups):
        pl.semaphore_signal(
            barrier, inc=1, device_id={"head": (me + step) % groups}, device_id_type=MESH
        )
    for step in (1, shards - 1):
        pl.semaphore_signal(
            barrier, inc=1, device_id={"seq": (seq + step) % shards}, device_id_type=MESH
        )

    heads = d_ref.shape[0]
    below = lax.broadcasted_iota(jnp.int32, (BLOCK, BLOCK), 0)
    above = lax.broadcasted_iota(jnp.int32, (BLOCK, BLOCK), 1)
    causal = below >= above
    ones = jnp.where(causal, 1.0, 0.0).astype(jnp.bfloat16)
    padding = jnp.zeros((LANES - heads, d_ref.shape[1]), jnp.float32)
    decay = jnp.concatenate([d_ref[...], padding], axis=0).T
    run1 = sum(mm(ones, part) for part in three(decay[:BLOCK]))
    run2 = sum(mm(ones, part) for part in three(decay[BLOCK:]))
    end1, end2 = run1[BLOCK - 1 :], run2[BLOCK - 1 :]
    mid1, mid2 = run1[BLOCK // 2 - 1 : BLOCK // 2], run2[BLOCK // 2 - 1 : BLOCK // 2]
    total = end1 + end2
    tables = jnp.concatenate(
        [
            jnp.exp(mid1 - run1),
            jnp.exp(mid2 - run2),
            jnp.exp(run1 - mid1),
            jnp.exp(run2 - mid2),
            jnp.exp(run2 + (end1 - mid1)),
        ],
        axis=0,
    )
    spread[...] = jnp.concatenate(two(tables), axis=1)
    grow[...] = jnp.concatenate(
        two(jnp.concatenate([jnp.exp(run1), jnp.exp(run2 + end1)], axis=0)), axis=1
    )
    gain = jnp.concatenate([g_ref[...], jnp.zeros((1, LANES - heads), jnp.float32)], axis=1)
    line = lax.broadcasted_iota(jnp.int32, (16, LANES), 0)
    picked = jnp.where(line == 1, jnp.exp(total - mid1), 0.0)
    picked = jnp.where(line == 2, jnp.exp(end2 - mid2), picked)
    picked = jnp.where(line == 3, gain, picked)
    rows[...] = jnp.concatenate(three(picked), axis=1)
    loss[me] = jnp.broadcast_to(jnp.exp(total), (8, LANES))

    b1, b2 = b_ref[:BLOCK], b_ref[BLOCK:]
    c1, c2 = c_ref[:BLOCK], c_ref[BLOCK:]
    last = ((1,), (1,))
    own1 = jnp.where(causal, full_mm(c1, b1, last), 0.0)
    own2 = jnp.where(causal, full_mm(c2, b2, last), 0.0)
    cross = full_mm(c2, b1, last)
    first[...] = left_side(jnp.concatenate([own1, cross, b1.T], axis=0))
    second[...] = left_side(jnp.concatenate([own2, b2.T], axis=0))
    readout[...] = left_side(c_ref[...])

    @pl.when(seq == 0)
    def _():
        sbuf[...] = jnp.zeros_like(sbuf)

    pl.semaphore_wait(barrier, groups + 1)
    for step in range(1, groups):
        share(step).start()

    def local(turn, carry):
        k, owner, chunk = at_turn(turn)
        x_copy(chunk).wait()
        x = xbuf[chunk]
        scale = mm(spread[...], expander(chunk, 2 * LANES, hpc, head_dim))
        lines = mm(rows[...], expander(chunk, 3 * LANES, hpc, head_dim))
        weighed = x * scale[: 2 * BLOCK]
        y1 = mm(first[...], right_side(weighed[:BLOCK]))
        y2 = mm(second[...], right_side(weighed[BLOCK:]))
        o_ref[:BLOCK, columns_of(chunk)] = y1[:BLOCK] * scale[2 * BLOCK : 3 * BLOCK] + lines[3:4] * x[:BLOCK]
        o_ref[BLOCK:, columns_of(chunk)] = (
            y2[:BLOCK] * scale[3 * BLOCK : 4 * BLOCK]
            + y1[BLOCK : 2 * BLOCK] * scale[4 * BLOCK :]
            + lines[3:4] * x[BLOCK:]
        )
        memory = y1[2 * BLOCK :] * lines[1:2] + y2[BLOCK:] * lines[2:3]

        @pl.when(owner == me)
        def _():
            rbuf[chunk] = memory

        @pl.when(owner != me)
        def _():
            mbuf[chunk] = memory
            forth(chunk, k, owner).start()

        return carry

    lax.fori_loop(0, chunks, local, 0)

    for step in range(1, groups):
        share_in((me + step) % groups).wait_recv()
    tall = -(-groups // 16) * 16
    line = lax.broadcasted_iota(jnp.int32, (tall, LANES), 0)
    losses = jnp.zeros((tall, LANES), jnp.float32)
    for j in range(groups):
        losses = jnp.where(line == j, loss[j, :1], losses)
    losses = jnp.concatenate(three(losses), axis=1)

    def link(k, carry):
        for step in range(1, groups):
            forth_in(((me + step) % groups) * per + k).wait_recv()
        wide = mm(losses, expander(me * per + k, 3 * LANES, hpc, head_dim))
        factors = [wide[j : j + 1] for j in range(groups)]
        shard = rbuf[k]
        shard_factor = factors[0]
        for j in range(1, groups):
            shard = factors[j] * shard + rbuf[j * per + k]
            shard_factor = shard_factor * factors[j]
        sout[k] = shard

        @pl.when(seq > 0)
        def _():
            chain(k).wait_recv()

        @pl.when(seq < shards - 1)
        def _():
            sout[k] = shard_factor * sbuf[k] + sout[k]
            chain(k).start()

        incoming = sbuf[k]
        for j in range(groups):
            slot = j * per + k
            here = rbuf[slot]
            rbuf[slot] = incoming

            @pl.when(me == j)
            def _():
                back[slot] = incoming

            @pl.when(me != j)
            def _():
                home(slot, k, j).start()

            incoming = factors[j] * incoming + here
        return carry

    lax.fori_loop(0, per, link, 0)

    def finish(turn, carry):
        k = turn // groups
        owner = (me + turn % groups) % groups
        chunk = owner * per + k

        @pl.when(owner != me)
        def _():
            home_in(chunk).wait_recv()

        carried = mm(readout[...], right_side(back[chunk]))
        growth = mm(grow[...], expander(chunk, 2 * LANES, hpc, head_dim))
        columns = columns_of(chunk)
        o_ref[:, columns] = o_ref[:, columns] + carried * growth
        return carry

    lax.fori_loop(0, chunks, finish, 0)

    def drain(chunk, carry):
        @pl.when(chunk // per != me)
        def _():
            forth_in(chunk).wait_send()
            home_in(chunk).wait_send()

        return carry

    lax.fori_loop(0, chunks, drain, 0)
    for step in range(1, groups):
        share(step).wait_send()

    @pl.when(seq < shards - 1)
    def _():
        def drain_chain(k, carry):
            chain(k).wait_send()
            return carry

        lax.fori_loop(0, per, drain_chain, 0)


def in_one(groups, shards, inputs, log_decay, input_map, output_map, skip_gain):
    tokens, width = inputs.shape
    state = input_map.shape[1]
    chunks = width // CHUNK
    per = chunks // groups
    head_dim = width // skip_gain.shape[0]
    vmem = pl.BlockSpec(memory_space=pltpu.VMEM)
    far = pl.BlockSpec(memory_space=pltpu.HBM)
    f32, bf16 = jnp.float32, jnp.bfloat16
    dma = pltpu.SemaphoreType.DMA
    return pl.pallas_call(
        functools.partial(whole_kernel, groups, shards, head_dim),
        out_shape=jax.ShapeDtypeStruct((tokens, width), f32),
        in_specs=[far, vmem, vmem, vmem, vmem],
        out_specs=vmem,
        scratch_shapes=[
            pltpu.VMEM((chunks, tokens, CHUNK), f32),
            pltpu.VMEM((chunks, state, CHUNK), f32),
            pltpu.VMEM((chunks, state, CHUNK), f32),
            pltpu.VMEM((per, state, CHUNK), f32),
            pltpu.VMEM((per, state, CHUNK), f32),
            pltpu.VMEM((chunks, state, CHUNK), f32),
            pltpu.VMEM((2 * BLOCK + state, 3 * BLOCK), bf16),
            pltpu.VMEM((BLOCK + state, 3 * BLOCK), bf16),
            pltpu.VMEM((tokens, 3 * state), bf16),
            pltpu.VMEM((5 * BLOCK, 2 * LANES), bf16),
            pltpu.VMEM((2 * BLOCK, 2 * LANES), bf16),
            pltpu.VMEM((16, 3 * LANES), bf16),
            pltpu.VMEM((groups, 8, LANES), f32),
            dma((chunks,)),
            dma((chunks,)),
            dma((chunks,)),
            dma((per,)),
            dma((per,)),
            dma((chunks,)),
            dma((chunks,)),
            dma((groups,)),
            dma((groups,)),
        ],
        compiler_params=pltpu.CompilerParams(
            collective_id=0, has_side_effects=True, vmem_limit_bytes=36 << 20
        ),
    )(
        *(
            pltpu.with_memory_space_constraint(operand, pltpu.HBM)
            for operand in (inputs, log_decay.T, input_map, output_map, skip_gain.reshape(1, -1))
        )
    )


def on_any(groups, shards, inputs, log_decay, input_map, output_map, skip_gain):
    tokens, width = inputs.shape
    heads = skip_gain.shape[0]
    head_dim = width // heads
    fits = (
        tokens == 2 * BLOCK
        and input_map.shape[1] == LANES
        and heads <= LANES
        and CHUNK % head_dim == 0
        and width % (groups * CHUNK) == 0
        and groups > 1
        and shards > 2
    )
    if fits:
        return in_one(groups, shards, inputs, log_decay, input_map, output_map, skip_gain)
    return on_device(inputs, log_decay, input_map, output_map, skip_gain)


def solution(mesh):
    in_specs = (
        P(("seq", "head"), None),
        P(("seq", "head"), None),
        P(("seq", "head"), None),
        P(("seq", "head"), None),
        P(),
    )
    out_specs = P(("seq", "head"), None)
    return jax.shard_map(
        functools.partial(on_any, mesh.shape["head"], mesh.shape["seq"]),
        mesh=mesh, in_specs=in_specs, out_specs=out_specs, check_vma=False,
    )
```

```python
import functools
import jax
import jax.numpy as jnp
from jax import lax
from jax.experimental import pallas as pl
from jax.experimental.pallas import tpu as pltpu
from jax.sharding import PartitionSpec as P

BLOCK = 128


PRECISE = lax.Precision.HIGHEST


def from_behind(value, axis, steps):
    count = lax.axis_size(axis)
    leading, last = (max(0, -steps), min(count, count - steps))
    return lax.ppermute(value, axis, [(source, source + steps) for source in range(leading, last)])


def scan_blocks(inputs, log_decay, input_map, output_map, head_dim):
    token_count = inputs.shape[0]
    width = inputs.shape[1]
    head_count = log_decay.shape[1]
    state_width = input_map.shape[1]
    blocks = token_count // BLOCK
    x_all = inputs.reshape(blocks, BLOCK, width)
    d_all = log_decay.reshape(blocks, BLOCK, head_count)
    b_all = input_map.reshape(blocks, BLOCK, state_width)
    c_all = output_map.reshape(blocks, BLOCK, state_width)
    running = jnp.cumsum(d_all, axis=1)
    run_heads = jnp.moveaxis(running, 2, 1)
    positions = jnp.arange(BLOCK)
    causal = positions[:, None] >= positions[None, :]
    spread = run_heads[:, :, :, None] - run_heads[:, :, None, :]
    decays = jnp.where(causal[None, None], jnp.exp(jnp.minimum(spread, 0.0)), 0.0)
    scores = jnp.einsum("bin,bjn->bij", c_all, b_all, precision=PRECISE)
    weighted = scores[:, None] * decays
    per_head = x_all.reshape(blocks, BLOCK, head_count, head_dim)
    within = jnp.einsum("bhij,bjhp->bihp", weighted, per_head, precision=PRECISE).reshape(
        blocks, BLOCK, width
    )
    closing = running[:, -1, :]
    remains = jnp.repeat(jnp.exp(closing[:, None, :] - running), head_dim, axis=2)
    own_state = jnp.einsum("bln,blw->bnw", b_all, x_all * remains, precision=PRECISE)
    totals = jnp.cumsum(closing, axis=0)
    before_total = totals - closing
    order = jnp.arange(blocks)
    earlier = order[:, None] > order[None, :]
    gap = before_total[:, None, :] - totals[None, :, :]
    link = jnp.where(earlier[:, :, None], jnp.exp(jnp.minimum(gap, 0.0)), 0.0)
    link_wide = jnp.repeat(link, head_dim, axis=2)
    entering = jnp.einsum("kjw,jnw->knw", link_wide, own_state, precision=PRECISE)
    final_weight = jnp.repeat(jnp.exp(totals[-1][None, :] - totals), head_dim, axis=1)
    memory = jnp.einsum("jw,jnw->nw", final_weight, own_state, precision=PRECISE)
    growth = jnp.repeat(jnp.exp(running), head_dim, axis=2)
    carried = jnp.einsum("bin,bnw->biw", c_all, entering, precision=PRECISE) * growth
    prefix = running + before_total[:, None, :]
    return (
        (within + carried).reshape(token_count, width),
        prefix.reshape(token_count, head_count),
        memory,
        totals[-1],
    )


def shard_chain(summed, memory, head_dim):
    factor = jnp.repeat(jnp.exp(summed), head_dim)[None, :]

    def advance(turn, incoming):
        return from_behind(factor * incoming + memory, "seq", 1)

    return lax.fori_loop(0, lax.axis_size("seq") - 1, advance, jnp.zeros_like(memory))


def on_device(inputs, log_decay, input_map, output_map, skip_gain):
    head_count = skip_gain.shape[0]
    head_dim = inputs.shape[1] // head_count
    state_width = input_map.shape[1]
    groups = lax.axis_size("head")
    local_heads = head_count // groups
    local_width = local_heads * head_dim
    results, prefix, memory, summed = scan_blocks(
        inputs, log_decay, input_map, output_map, head_dim
    )
    got_sum, got_state = (
        lax.all_to_all(
            summed.reshape(1, groups, local_heads), "head", split_axis=1, concat_axis=1, tiled=True
        ),
        lax.all_to_all(
            memory.reshape(state_width, groups, local_width),
            "head",
            split_axis=1,
            concat_axis=1,
            tiled=True,
        ),
    )

    def within_shard(carry, item):
        total_decay, total_state = carry
        decay_here, state_here = item
        scale_now = jnp.repeat(jnp.exp(decay_here), head_dim)[None, :]
        return ((total_decay + decay_here, scale_now * total_state + state_here), carry)

    start_carry = (
        jnp.zeros((local_heads,), jnp.float32),
        jnp.zeros((state_width, local_width), jnp.float32),
    )
    (shard_decay, shard_state), (before_decay, before_state) = lax.scan(
        within_shard, start_carry, (got_sum[0], jnp.moveaxis(got_state, 1, 0))
    )
    incoming = shard_chain(shard_decay, shard_state, head_dim)
    per_source = (
        jnp.repeat(jnp.exp(before_decay), head_dim, axis=1)[:, None, :] * incoming[None]
        + before_state
    )
    back = lax.all_to_all(
        jnp.moveaxis(per_source, 0, 1), "head", split_axis=1, concat_axis=1, tiled=True
    )
    arrived = back.reshape(state_width, head_count * head_dim)
    returned = results + jnp.dot(output_map, arrived, precision=PRECISE) * jnp.repeat(
        jnp.exp(prefix), head_dim, axis=1
    )
    return returned + inputs * jnp.repeat(skip_gain, head_dim)[None, :]


MESH = pl.DeviceIdType.MESH
CHUNK = 256
LANES = 128


def two(value):
    high = value.astype(jnp.bfloat16)
    return high, (value - high.astype(jnp.float32)).astype(jnp.bfloat16)


def three(value):
    high = value.astype(jnp.bfloat16)
    rest = value - high.astype(jnp.float32)
    middle = rest.astype(jnp.bfloat16)
    return high, middle, (rest - middle.astype(jnp.float32)).astype(jnp.bfloat16)


def left_side(value):
    high, low = two(value)
    return jnp.concatenate([high, high, low], axis=1)


def right_side(value):
    high, low = two(value)
    return jnp.concatenate([high, low, high], axis=0)


def mm(a, b):
    return jnp.dot(a, b, preferred_element_type=jnp.float32)


def full_mm(a, b, dims):
    return lax.dot_general(
        a, b, (dims, ((), ())), precision=PRECISE, preferred_element_type=jnp.float32
    )


def expander(chunk, depth, heads_per_chunk, head_dim):
    row = lax.broadcasted_iota(jnp.int32, (depth, CHUNK), 0) & (LANES - 1)
    column = lax.broadcasted_iota(jnp.int32, (depth, CHUNK), 1) // head_dim
    hit = row == column + chunk * heads_per_chunk
    return jnp.where(hit, 1.0, 0.0).astype(jnp.bfloat16)


def whole_kernel(
    groups, shards, head_dim,
    x_hbm, d_hbm, b_hbm, c_hbm, g_hbm, o_ref,
    d_ref, b_ref, c_ref, g_ref, xbuf, mbuf, rbuf, sbuf, sout, back,
    state1, state2, first, second, readout, lift, spread, grow, rows, loss,
    isem, xsem, fsend, frecv, csend, crecv, bsend, brecv, lsend, lrecv,
):
    seq = lax.axis_index("seq")
    me = lax.axis_index("head")
    chunks = xbuf.shape[0]
    per = chunks // groups
    state = b_ref.shape[1]
    hpc = CHUNK // head_dim

    def x_copy(chunk):
        columns = pl.ds(pl.multiple_of(chunk * CHUNK, CHUNK), CHUNK)
        return pltpu.make_async_copy(x_hbm.at[:, columns], xbuf.at[chunk], xsem.at[chunk])

    def columns_of(chunk):
        return pl.ds(pl.multiple_of(chunk * CHUNK, CHUNK), CHUNK)

    def share(step):
        return pltpu.make_async_remote_copy(
            src_ref=loss.at[me],
            dst_ref=loss.at[me],
            send_sem=lsend.at[step],
            recv_sem=lrecv.at[me],
            device_id={"head": (me + step) % groups},
            device_id_type=MESH,
        )

    def share_in(source):
        return pltpu.make_async_remote_copy(
            src_ref=loss.at[source],
            dst_ref=loss.at[source],
            send_sem=lsend.at[0],
            recv_sem=lrecv.at[source],
            device_id={"head": (me + 1) % groups},
            device_id_type=MESH,
        )

    def at_turn(turn):
        k = turn // groups
        owner = (me + 1 + turn % groups) % groups
        return k, owner, owner * per + k

    def forth(chunk, k, owner):
        return pltpu.make_async_remote_copy(
            src_ref=mbuf.at[chunk],
            dst_ref=rbuf.at[me * per + k],
            send_sem=fsend.at[chunk],
            recv_sem=frecv.at[me * per + k],
            device_id={"head": owner},
            device_id_type=MESH,
        )

    def forth_in(slot):
        return pltpu.make_async_remote_copy(
            src_ref=mbuf.at[slot],
            dst_ref=rbuf.at[slot],
            send_sem=fsend.at[slot],
            recv_sem=frecv.at[slot],
            device_id={"head": (me + 1) % groups},
            device_id_type=MESH,
        )

    def chain(k):
        return pltpu.make_async_remote_copy(
            src_ref=sout.at[k],
            dst_ref=sbuf.at[k],
            send_sem=csend.at[k],
            recv_sem=crecv.at[k],
            device_id={"seq": (seq + 1) % shards},
            device_id_type=MESH,
        )

    def home(slot, k, target):
        return pltpu.make_async_remote_copy(
            src_ref=rbuf.at[slot],
            dst_ref=back.at[me * per + k],
            send_sem=bsend.at[slot],
            recv_sem=brecv.at[me * per + k],
            device_id={"head": target},
            device_id_type=MESH,
        )

    def home_in(slot):
        return pltpu.make_async_remote_copy(
            src_ref=rbuf.at[slot],
            dst_ref=back.at[slot],
            send_sem=bsend.at[slot],
            recv_sem=brecv.at[slot],
            device_id={"head": (me + 1) % groups},
            device_id_type=MESH,
        )

    def load(turn, carry):
        x_copy(at_turn(turn)[2]).start()
        return carry

    barrier = pltpu.get_barrier_semaphore()
    for step in range(1, groups):
        pl.semaphore_signal(
            barrier, inc=1, device_id={"head": (me + step) % groups}, device_id_type=MESH
        )
    for step in (1, shards - 1):
        pl.semaphore_signal(
            barrier, inc=1, device_id={"seq": (seq + step) % shards}, device_id_type=MESH
        )

    pairs = ((d_hbm, d_ref), (b_hbm, b_ref), (g_hbm, g_ref), (c_hbm, c_ref))
    small = [pltpu.make_async_copy(*pair, isem.at[i]) for i, pair in enumerate(pairs)]
    small[0].start()
    small[1].start()
    small[2].start()
    lax.fori_loop(0, chunks, load, 0)
    small[3].start()

    heads = d_ref.shape[0]
    below = lax.broadcasted_iota(jnp.int32, (BLOCK, BLOCK), 0)
    above = lax.broadcasted_iota(jnp.int32, (BLOCK, BLOCK), 1)
    causal = below >= above
    ones = jnp.where(causal, 1.0, 0.0).astype(jnp.bfloat16)
    small[0].wait()
    padding = jnp.zeros((LANES - heads, d_ref.shape[1]), jnp.float32)
    decay = jnp.concatenate([d_ref[...], padding], axis=0).T
    run1 = sum(mm(ones, part) for part in three(decay[:BLOCK]))
    run2 = sum(mm(ones, part) for part in three(decay[BLOCK:]))
    end1, end2 = run1[BLOCK - 1 :], run2[BLOCK - 1 :]
    mid1, mid2 = run1[BLOCK // 2 - 1 : BLOCK // 2], run2[BLOCK // 2 - 1 : BLOCK // 2]
    total = end1 + end2
    up = jnp.concatenate([jnp.exp(mid1 - run1), jnp.exp(mid2 - run2)], axis=0)
    lift[...] = jnp.concatenate(two(up), axis=1)
    small[2].wait()
    gain = jnp.concatenate([g_ref[...], jnp.zeros((1, LANES - heads), jnp.float32)], axis=1)
    line = lax.broadcasted_iota(jnp.int32, (16, LANES), 0)
    picked = jnp.where(line == 1, jnp.exp(total - mid1), 0.0)
    picked = jnp.where(line == 2, jnp.exp(end2 - mid2), picked)
    picked = jnp.where(line == 3, gain, picked)
    rows[...] = jnp.concatenate(three(picked), axis=1)
    loss[me] = jnp.broadcast_to(jnp.exp(total), (8, LANES))
    small[1].wait()
    b1, b2 = b_ref[:BLOCK], b_ref[BLOCK:]
    state1[...] = left_side(b1.T)
    state2[...] = left_side(b2.T)

    @pl.when(seq == 0)
    def _():
        sbuf[...] = jnp.zeros_like(sbuf)

    pl.semaphore_wait(barrier, groups + 1)
    for step in range(1, groups):
        share(step).start()

    def weighed(chunk):
        scale = mm(lift[...], expander(chunk, 2 * LANES, hpc, head_dim))
        value = xbuf[chunk] * scale
        return right_side(value[:BLOCK]), right_side(value[BLOCK:])

    def send(turn, carry):
        k, owner, chunk = at_turn(turn)
        x_copy(chunk).wait()
        w1, w2 = weighed(chunk)
        lines = mm(rows[...], expander(chunk, 3 * LANES, hpc, head_dim))
        memory = mm(state1[...], w1) * lines[1:2] + mm(state2[...], w2) * lines[2:3]

        @pl.when(owner == me)
        def _():
            rbuf[chunk] = memory

        @pl.when(owner != me)
        def _():
            mbuf[chunk] = memory
            forth(chunk, k, owner).start()

        return carry

    lax.fori_loop(0, chunks, send, 0)

    down = jnp.concatenate(
        [
            jnp.exp(run1 - mid1),
            jnp.exp(run2 - mid2),
            jnp.exp(run2 + (end1 - mid1)),
        ],
        axis=0,
    )
    spread[...] = jnp.concatenate(two(down), axis=1)
    grow[...] = jnp.concatenate(
        two(jnp.concatenate([jnp.exp(run1), jnp.exp(run2 + end1)], axis=0)), axis=1
    )
    small[3].wait()
    c1, c2 = c_ref[:BLOCK], c_ref[BLOCK:]
    last = ((1,), (1,))
    own1 = jnp.where(causal, full_mm(c1, b1, last), 0.0)
    own2 = jnp.where(causal, full_mm(c2, b2, last), 0.0)
    cross = full_mm(c2, b1, last)
    first[...] = left_side(jnp.concatenate([own1, cross], axis=0))
    second[...] = left_side(own2)
    readout[...] = left_side(c_ref[...])

    def local(turn, carry):
        k, owner, chunk = at_turn(turn)
        w1, w2 = weighed(chunk)
        scale = mm(spread[...], expander(chunk, 2 * LANES, hpc, head_dim))
        lines = mm(rows[...], expander(chunk, 3 * LANES, hpc, head_dim))
        y1 = mm(first[...], w1)
        y2 = mm(second[...], w2)
        columns = columns_of(chunk)
        o_ref[:BLOCK, columns] = y1[:BLOCK] * scale[:BLOCK] + lines[3:4] * xbuf[chunk, :BLOCK]
        o_ref[BLOCK:, columns] = (
            y2 * scale[BLOCK : 2 * BLOCK]
            + y1[BLOCK:] * scale[2 * BLOCK :]
            + lines[3:4] * xbuf[chunk, BLOCK:]
        )
        return carry

    lax.fori_loop(0, groups, local, 0)
    for step in range(1, groups):
        share_in((me + step) % groups).wait_recv()
    tall = -(-groups // 16) * 16
    line = lax.broadcasted_iota(jnp.int32, (tall, LANES), 0)
    losses = jnp.zeros((tall, LANES), jnp.float32)
    for j in range(groups):
        losses = jnp.where(line == j, loss[j, :1], losses)
    losses = jnp.concatenate(three(losses), axis=1)

    def link(k, carry):
        lax.fori_loop(
            jnp.minimum((k + 1) * groups, chunks), jnp.minimum((k + 2) * groups, chunks), local, 0
        )
        for step in range(1, groups):
            forth_in(((me + step) % groups) * per + k).wait_recv()
        wide = mm(losses, expander(me * per + k, 3 * LANES, hpc, head_dim))
        factors = [wide[j : j + 1] for j in range(groups)]
        shard = rbuf[k]
        shard_factor = factors[0]
        for j in range(1, groups):
            shard = factors[j] * shard + rbuf[j * per + k]
            shard_factor = shard_factor * factors[j]
        sout[k] = shard

        @pl.when(seq > 0)
        def _():
            chain(k).wait_recv()

        @pl.when(seq < shards - 1)
        def _():
            sout[k] = shard_factor * sbuf[k] + sout[k]
            chain(k).start()

        incoming = sbuf[k]
        for j in range(groups):
            slot = j * per + k
            here = rbuf[slot]
            rbuf[slot] = incoming

            @pl.when(me == j)
            def _():
                back[slot] = incoming

            @pl.when(me != j)
            def _():
                home(slot, k, j).start()

            incoming = factors[j] * incoming + here
        return carry

    lax.fori_loop(0, per, link, 0)

    def finish(turn, carry):
        k = turn // groups
        owner = (me + turn % groups) % groups
        chunk = owner * per + k

        @pl.when(owner != me)
        def _():
            home_in(chunk).wait_recv()

        carried = mm(readout[...], right_side(back[chunk]))
        growth = mm(grow[...], expander(chunk, 2 * LANES, hpc, head_dim))
        columns = columns_of(chunk)
        o_ref[:, columns] = o_ref[:, columns] + carried * growth
        return carry

    lax.fori_loop(0, chunks, finish, 0)

    def drain(chunk, carry):
        @pl.when(chunk // per != me)
        def _():
            forth_in(chunk).wait_send()
            home_in(chunk).wait_send()

        return carry

    lax.fori_loop(0, chunks, drain, 0)
    for step in range(1, groups):
        share(step).wait_send()

    @pl.when(seq < shards - 1)
    def _():
        def drain_chain(k, carry):
            chain(k).wait_send()
            return carry

        lax.fori_loop(0, per, drain_chain, 0)


def in_one(groups, shards, inputs, log_decay, input_map, output_map, skip_gain):
    tokens, width = inputs.shape
    state = input_map.shape[1]
    chunks = width // CHUNK
    per = chunks // groups
    head_dim = width // skip_gain.shape[0]
    vmem = pl.BlockSpec(memory_space=pltpu.VMEM)
    far = pl.BlockSpec(memory_space=pltpu.HBM)
    f32, bf16 = jnp.float32, jnp.bfloat16
    dma = pltpu.SemaphoreType.DMA
    return pl.pallas_call(
        functools.partial(whole_kernel, groups, shards, head_dim),
        out_shape=jax.ShapeDtypeStruct((tokens, width), f32),
        in_specs=[far] * 5,
        out_specs=vmem,
        scratch_shapes=[
            pltpu.VMEM(log_decay.shape[::-1], f32),
            pltpu.VMEM(input_map.shape, f32),
            pltpu.VMEM(output_map.shape, f32),
            pltpu.VMEM((1, skip_gain.shape[0]), f32),
            pltpu.VMEM((chunks, tokens, CHUNK), f32),
            pltpu.VMEM((chunks, state, CHUNK), f32),
            pltpu.VMEM((chunks, state, CHUNK), f32),
            pltpu.VMEM((per, state, CHUNK), f32),
            pltpu.VMEM((per, state, CHUNK), f32),
            pltpu.VMEM((chunks, state, CHUNK), f32),
            pltpu.VMEM((state, 3 * BLOCK), bf16),
            pltpu.VMEM((state, 3 * BLOCK), bf16),
            pltpu.VMEM((2 * BLOCK, 3 * BLOCK), bf16),
            pltpu.VMEM((BLOCK, 3 * BLOCK), bf16),
            pltpu.VMEM((tokens, 3 * state), bf16),
            pltpu.VMEM((2 * BLOCK, 2 * LANES), bf16),
            pltpu.VMEM((3 * BLOCK, 2 * LANES), bf16),
            pltpu.VMEM((2 * BLOCK, 2 * LANES), bf16),
            pltpu.VMEM((16, 3 * LANES), bf16),
            pltpu.VMEM((groups, 8, LANES), f32),
            dma((4,)),
            dma((chunks,)),
            dma((chunks,)),
            dma((chunks,)),
            dma((per,)),
            dma((per,)),
            dma((chunks,)),
            dma((chunks,)),
            dma((groups,)),
            dma((groups,)),
        ],
        compiler_params=pltpu.CompilerParams(
            collective_id=0, has_side_effects=True, vmem_limit_bytes=36 << 20
        ),
    )(
        *(
            pltpu.with_memory_space_constraint(operand, pltpu.HBM)
            for operand in (inputs, log_decay.T, input_map, output_map, skip_gain.reshape(1, -1))
        )
    )


def on_any(groups, shards, inputs, log_decay, input_map, output_map, skip_gain):
    tokens, width = inputs.shape
    heads = skip_gain.shape[0]
    head_dim = width // heads
    fits = (
        tokens == 2 * BLOCK
        and input_map.shape[1] == LANES
        and heads <= LANES
        and CHUNK % head_dim == 0
        and width % (groups * CHUNK) == 0
        and groups > 1
        and shards > 2
    )
    if fits:
        return in_one(groups, shards, inputs, log_decay, input_map, output_map, skip_gain)
    return on_device(inputs, log_decay, input_map, output_map, skip_gain)


def solution(mesh):
    in_specs = (
        P(("seq", "head"), None),
        P(("seq", "head"), None),
        P(("seq", "head"), None),
        P(("seq", "head"), None),
        P(),
    )
    out_specs = P(("seq", "head"), None)
    return jax.shard_map(
        functools.partial(on_any, mesh.shape["head"], mesh.shape["seq"]),
        mesh=mesh, in_specs=in_specs, out_specs=out_specs, check_vma=False,
    )
```

```python
import functools
import jax
import jax.numpy as jnp
from jax import lax
from jax.experimental import pallas as pl
from jax.experimental.pallas import tpu as pltpu
from jax.sharding import PartitionSpec as P

BLOCK = 128


PRECISE = lax.Precision.HIGHEST


def from_behind(value, axis, steps):
    count = lax.axis_size(axis)
    leading, last = (max(0, -steps), min(count, count - steps))
    return lax.ppermute(value, axis, [(source, source + steps) for source in range(leading, last)])


def scan_blocks(inputs, log_decay, input_map, output_map, head_dim):
    token_count = inputs.shape[0]
    width = inputs.shape[1]
    head_count = log_decay.shape[1]
    state_width = input_map.shape[1]
    blocks = token_count // BLOCK
    x_all = inputs.reshape(blocks, BLOCK, width)
    d_all = log_decay.reshape(blocks, BLOCK, head_count)
    b_all = input_map.reshape(blocks, BLOCK, state_width)
    c_all = output_map.reshape(blocks, BLOCK, state_width)
    running = jnp.cumsum(d_all, axis=1)
    run_heads = jnp.moveaxis(running, 2, 1)
    positions = jnp.arange(BLOCK)
    causal = positions[:, None] >= positions[None, :]
    spread = run_heads[:, :, :, None] - run_heads[:, :, None, :]
    decays = jnp.where(causal[None, None], jnp.exp(jnp.minimum(spread, 0.0)), 0.0)
    scores = jnp.einsum("bin,bjn->bij", c_all, b_all, precision=PRECISE)
    weighted = scores[:, None] * decays
    per_head = x_all.reshape(blocks, BLOCK, head_count, head_dim)
    within = jnp.einsum("bhij,bjhp->bihp", weighted, per_head, precision=PRECISE).reshape(
        blocks, BLOCK, width
    )
    closing = running[:, -1, :]
    remains = jnp.repeat(jnp.exp(closing[:, None, :] - running), head_dim, axis=2)
    own_state = jnp.einsum("bln,blw->bnw", b_all, x_all * remains, precision=PRECISE)
    totals = jnp.cumsum(closing, axis=0)
    before_total = totals - closing
    order = jnp.arange(blocks)
    earlier = order[:, None] > order[None, :]
    gap = before_total[:, None, :] - totals[None, :, :]
    link = jnp.where(earlier[:, :, None], jnp.exp(jnp.minimum(gap, 0.0)), 0.0)
    link_wide = jnp.repeat(link, head_dim, axis=2)
    entering = jnp.einsum("kjw,jnw->knw", link_wide, own_state, precision=PRECISE)
    final_weight = jnp.repeat(jnp.exp(totals[-1][None, :] - totals), head_dim, axis=1)
    memory = jnp.einsum("jw,jnw->nw", final_weight, own_state, precision=PRECISE)
    growth = jnp.repeat(jnp.exp(running), head_dim, axis=2)
    carried = jnp.einsum("bin,bnw->biw", c_all, entering, precision=PRECISE) * growth
    prefix = running + before_total[:, None, :]
    return (
        (within + carried).reshape(token_count, width),
        prefix.reshape(token_count, head_count),
        memory,
        totals[-1],
    )


def shard_chain(summed, memory, head_dim):
    factor = jnp.repeat(jnp.exp(summed), head_dim)[None, :]

    def advance(turn, incoming):
        return from_behind(factor * incoming + memory, "seq", 1)

    return lax.fori_loop(0, lax.axis_size("seq") - 1, advance, jnp.zeros_like(memory))


def on_device(inputs, log_decay, input_map, output_map, skip_gain):
    head_count = skip_gain.shape[0]
    head_dim = inputs.shape[1] // head_count
    state_width = input_map.shape[1]
    groups = lax.axis_size("head")
    local_heads = head_count // groups
    local_width = local_heads * head_dim
    results, prefix, memory, summed = scan_blocks(
        inputs, log_decay, input_map, output_map, head_dim
    )
    got_sum, got_state = (
        lax.all_to_all(
            summed.reshape(1, groups, local_heads), "head", split_axis=1, concat_axis=1, tiled=True
        ),
        lax.all_to_all(
            memory.reshape(state_width, groups, local_width),
            "head",
            split_axis=1,
            concat_axis=1,
            tiled=True,
        ),
    )

    def within_shard(carry, item):
        total_decay, total_state = carry
        decay_here, state_here = item
        scale_now = jnp.repeat(jnp.exp(decay_here), head_dim)[None, :]
        return ((total_decay + decay_here, scale_now * total_state + state_here), carry)

    start_carry = (
        jnp.zeros((local_heads,), jnp.float32),
        jnp.zeros((state_width, local_width), jnp.float32),
    )
    (shard_decay, shard_state), (before_decay, before_state) = lax.scan(
        within_shard, start_carry, (got_sum[0], jnp.moveaxis(got_state, 1, 0))
    )
    incoming = shard_chain(shard_decay, shard_state, head_dim)
    per_source = (
        jnp.repeat(jnp.exp(before_decay), head_dim, axis=1)[:, None, :] * incoming[None]
        + before_state
    )
    back = lax.all_to_all(
        jnp.moveaxis(per_source, 0, 1), "head", split_axis=1, concat_axis=1, tiled=True
    )
    arrived = back.reshape(state_width, head_count * head_dim)
    returned = results + jnp.dot(output_map, arrived, precision=PRECISE) * jnp.repeat(
        jnp.exp(prefix), head_dim, axis=1
    )
    return returned + inputs * jnp.repeat(skip_gain, head_dim)[None, :]


MESH = pl.DeviceIdType.MESH
CHUNK = 256
LANES = 128


def two(value):
    high = value.astype(jnp.bfloat16)
    return high, (value - high.astype(jnp.float32)).astype(jnp.bfloat16)


def three(value):
    high = value.astype(jnp.bfloat16)
    rest = value - high.astype(jnp.float32)
    middle = rest.astype(jnp.bfloat16)
    return high, middle, (rest - middle.astype(jnp.float32)).astype(jnp.bfloat16)


def left_side(value):
    high, low = two(value)
    return jnp.concatenate([high, high, low], axis=1)


def right_side(value):
    high, low = two(value)
    return jnp.concatenate([high, low, high], axis=0)


def mm(a, b):
    return jnp.dot(a, b, preferred_element_type=jnp.float32)


def full_mm(a, b, dims):
    return lax.dot_general(
        a, b, (dims, ((), ())), precision=PRECISE, preferred_element_type=jnp.float32
    )


def expander(chunk, depth, heads_per_chunk, head_dim):
    row = lax.broadcasted_iota(jnp.int32, (depth, CHUNK), 0) & (LANES - 1)
    column = lax.broadcasted_iota(jnp.int32, (depth, CHUNK), 1) // head_dim
    hit = row == column + chunk * heads_per_chunk
    return jnp.where(hit, 1.0, 0.0).astype(jnp.bfloat16)


def whole_kernel(
    groups, shards, head_dim,
    x_hbm, d_hbm, b_hbm, c_hbm, g_hbm, o_ref, late, grow, readout,
    d_ref, b_ref, c_ref, g_ref, xbuf, mbuf, rbuf, sbuf, sout, back,
    state1, state2, first, second, lift, spread, rows, loss,
    isem, xsem, fsend, frecv, csend, crecv, bsend, brecv, lsend, lrecv,
):
    seq = lax.axis_index("seq")
    me = lax.axis_index("head")
    chunks = xbuf.shape[0]
    per = chunks // groups
    state = b_ref.shape[1]
    hpc = CHUNK // head_dim

    def x_copy(chunk):
        columns = pl.ds(pl.multiple_of(chunk * CHUNK, CHUNK), CHUNK)
        return pltpu.make_async_copy(x_hbm.at[:, columns], xbuf.at[chunk], xsem.at[chunk])

    def columns_of(chunk):
        return pl.ds(pl.multiple_of(chunk * CHUNK, CHUNK), CHUNK)

    def share(step):
        return pltpu.make_async_remote_copy(
            src_ref=loss.at[me],
            dst_ref=loss.at[me],
            send_sem=lsend.at[step],
            recv_sem=lrecv.at[me],
            device_id={"head": (me + step) % groups},
            device_id_type=MESH,
        )

    def share_in(source):
        return pltpu.make_async_remote_copy(
            src_ref=loss.at[source],
            dst_ref=loss.at[source],
            send_sem=lsend.at[0],
            recv_sem=lrecv.at[source],
            device_id={"head": (me + 1) % groups},
            device_id_type=MESH,
        )

    def at_turn(turn):
        k = turn // groups
        owner = (me + 1 + turn % groups) % groups
        return k, owner, owner * per + k

    def forth(chunk, k, owner):
        return pltpu.make_async_remote_copy(
            src_ref=mbuf.at[chunk],
            dst_ref=rbuf.at[me * per + k],
            send_sem=fsend.at[chunk],
            recv_sem=frecv.at[me * per + k],
            device_id={"head": owner},
            device_id_type=MESH,
        )

    def forth_in(slot):
        return pltpu.make_async_remote_copy(
            src_ref=mbuf.at[slot],
            dst_ref=rbuf.at[slot],
            send_sem=fsend.at[slot],
            recv_sem=frecv.at[slot],
            device_id={"head": (me + 1) % groups},
            device_id_type=MESH,
        )

    def chain(k):
        return pltpu.make_async_remote_copy(
            src_ref=sout.at[k],
            dst_ref=sbuf.at[k],
            send_sem=csend.at[k],
            recv_sem=crecv.at[k],
            device_id={"seq": (seq + 1) % shards},
            device_id_type=MESH,
        )

    def home(slot, k, target):
        return pltpu.make_async_remote_copy(
            src_ref=rbuf.at[slot],
            dst_ref=back.at[me * per + k],
            send_sem=bsend.at[slot],
            recv_sem=brecv.at[me * per + k],
            device_id={"head": target},
            device_id_type=MESH,
        )

    def home_in(slot):
        return pltpu.make_async_remote_copy(
            src_ref=rbuf.at[slot],
            dst_ref=back.at[slot],
            send_sem=bsend.at[slot],
            recv_sem=brecv.at[slot],
            device_id={"head": (me + 1) % groups},
            device_id_type=MESH,
        )

    def load(turn, carry):
        x_copy(at_turn(turn)[2]).start()
        return carry

    barrier = pltpu.get_barrier_semaphore()
    for step in range(1, groups):
        pl.semaphore_signal(
            barrier, inc=1, device_id={"head": (me + step) % groups}, device_id_type=MESH
        )
    for step in (1, shards - 1):
        pl.semaphore_signal(
            barrier, inc=1, device_id={"seq": (seq + step) % shards}, device_id_type=MESH
        )

    pairs = ((d_hbm, d_ref), (b_hbm, b_ref), (g_hbm, g_ref), (c_hbm, c_ref))
    small = [pltpu.make_async_copy(*pair, isem.at[i]) for i, pair in enumerate(pairs)]
    small[0].start()
    small[1].start()
    small[2].start()
    lax.fori_loop(0, chunks, load, 0)
    small[3].start()

    heads = d_ref.shape[0]
    below = lax.broadcasted_iota(jnp.int32, (BLOCK, BLOCK), 0)
    above = lax.broadcasted_iota(jnp.int32, (BLOCK, BLOCK), 1)
    causal = below >= above
    ones = jnp.where(causal, 1.0, 0.0).astype(jnp.bfloat16)
    small[0].wait()
    padding = jnp.zeros((LANES - heads, d_ref.shape[1]), jnp.float32)
    decay = jnp.concatenate([d_ref[...], padding], axis=0).T
    run1 = sum(mm(ones, part) for part in three(decay[:BLOCK]))
    run2 = sum(mm(ones, part) for part in three(decay[BLOCK:]))
    end1, end2 = run1[BLOCK - 1 :], run2[BLOCK - 1 :]
    mid1, mid2 = run1[BLOCK // 2 - 1 : BLOCK // 2], run2[BLOCK // 2 - 1 : BLOCK // 2]
    total = end1 + end2
    up = jnp.concatenate([jnp.exp(mid1 - run1), jnp.exp(mid2 - run2)], axis=0)
    lift[...] = jnp.concatenate(two(up), axis=1)
    small[2].wait()
    gain = jnp.concatenate([g_ref[...], jnp.zeros((1, LANES - heads), jnp.float32)], axis=1)
    line = lax.broadcasted_iota(jnp.int32, (16, LANES), 0)
    picked = jnp.where(line == 1, jnp.exp(total - mid1), 0.0)
    picked = jnp.where(line == 2, jnp.exp(end2 - mid2), picked)
    picked = jnp.where(line == 3, gain, picked)
    rows[...] = jnp.concatenate(three(picked), axis=1)
    loss[me] = jnp.broadcast_to(jnp.exp(total), (8, LANES))
    small[1].wait()
    b1, b2 = b_ref[:BLOCK], b_ref[BLOCK:]
    state1[...] = left_side(b1.T)
    state2[...] = left_side(b2.T)

    @pl.when(seq == 0)
    def _():
        sbuf[...] = jnp.zeros_like(sbuf)

    pl.semaphore_wait(barrier, groups + 1)
    for step in range(1, groups):
        share(step).start()

    def weighed(chunk):
        scale = mm(lift[...], expander(chunk, 2 * LANES, hpc, head_dim))
        value = xbuf[chunk] * scale
        return right_side(value[:BLOCK]), right_side(value[BLOCK:])

    def send(turn, carry):
        k, owner, chunk = at_turn(turn)
        x_copy(chunk).wait()
        w1, w2 = weighed(chunk)
        lines = mm(rows[...], expander(chunk, 3 * LANES, hpc, head_dim))
        memory = mm(state1[...], w1) * lines[1:2] + mm(state2[...], w2) * lines[2:3]

        @pl.when(owner == me)
        def _():
            rbuf[chunk] = memory

        @pl.when(owner != me)
        def _():
            mbuf[chunk] = memory
            forth(chunk, k, owner).start()

        return carry

    lax.fori_loop(0, chunks, send, 0)

    down = jnp.concatenate(
        [
            jnp.exp(run1 - mid1),
            jnp.exp(run2 - mid2),
            jnp.exp(run2 + (end1 - mid1)),
        ],
        axis=0,
    )
    spread[...] = jnp.concatenate(two(down), axis=1)
    grow[...] = jnp.concatenate(
        two(jnp.concatenate([jnp.exp(run1), jnp.exp(run2 + end1)], axis=0)), axis=1
    )
    small[3].wait()
    c1, c2 = c_ref[:BLOCK], c_ref[BLOCK:]
    last = ((1,), (1,))
    own1 = jnp.where(causal, full_mm(c1, b1, last), 0.0)
    own2 = jnp.where(causal, full_mm(c2, b2, last), 0.0)
    cross = full_mm(c2, b1, last)
    first[...] = left_side(jnp.concatenate([own1, cross], axis=0))
    second[...] = left_side(own2)
    readout[...] = left_side(c_ref[...])

    def local(turn, carry):
        k, owner, chunk = at_turn(turn)
        w1, w2 = weighed(chunk)
        scale = mm(spread[...], expander(chunk, 2 * LANES, hpc, head_dim))
        lines = mm(rows[...], expander(chunk, 3 * LANES, hpc, head_dim))
        y1 = mm(first[...], w1)
        y2 = mm(second[...], w2)
        columns = columns_of(chunk)
        o_ref[:BLOCK, columns] = y1[:BLOCK] * scale[:BLOCK] + lines[3:4] * xbuf[chunk, :BLOCK]
        o_ref[BLOCK:, columns] = (
            y2 * scale[BLOCK : 2 * BLOCK]
            + y1[BLOCK:] * scale[2 * BLOCK :]
            + lines[3:4] * xbuf[chunk, BLOCK:]
        )
        return carry

    lax.fori_loop(0, groups, local, 0)
    for step in range(1, groups):
        share_in((me + step) % groups).wait_recv()
    tall = -(-groups // 16) * 16
    line = lax.broadcasted_iota(jnp.int32, (tall, LANES), 0)
    losses = jnp.zeros((tall, LANES), jnp.float32)
    for j in range(groups):
        losses = jnp.where(line == j, loss[j, :1], losses)
    losses = jnp.concatenate(three(losses), axis=1)

    def link(k, carry):
        lax.fori_loop(
            jnp.minimum((k + 1) * groups, chunks), jnp.minimum((k + 2) * groups, chunks), local, 0
        )
        for step in range(1, groups):
            forth_in(((me + step) % groups) * per + k).wait_recv()
        wide = mm(losses, expander(me * per + k, 3 * LANES, hpc, head_dim))
        factors = [wide[j : j + 1] for j in range(groups)]
        shard = rbuf[k]
        shard_factor = factors[0]
        for j in range(1, groups):
            shard = factors[j] * shard + rbuf[j * per + k]
            shard_factor = shard_factor * factors[j]
        sout[k] = shard

        @pl.when(seq > 0)
        def _():
            chain(k).wait_recv()

        @pl.when(seq < shards - 1)
        def _():
            sout[k] = shard_factor * sbuf[k] + sout[k]
            chain(k).start()

        incoming = sbuf[k]
        for j in range(groups):
            slot = j * per + k
            here = rbuf[slot]
            rbuf[slot] = incoming

            @pl.when(me == j)
            def _():
                back[slot] = incoming

            @pl.when(me != j)
            def _():
                home(slot, k, j).start()

            incoming = factors[j] * incoming + here
        return carry

    lax.fori_loop(0, per, link, 0)

    def finish(turn, carry):
        k = turn // groups
        owner = (me + turn % groups) % groups
        chunk = owner * per + k

        @pl.when(owner != me)
        def _():
            home_in(chunk).wait_recv()

        carried = mm(readout[...], right_side(back[chunk]))
        growth = mm(grow[...], expander(chunk, 2 * LANES, hpc, head_dim))
        columns = columns_of(chunk)
        o_ref[:, columns] = o_ref[:, columns] + carried * growth
        return carry

    lax.fori_loop(0, chunks - groups, finish, 0)

    def arrive(turn, carry):
        owner = (me + turn) % groups
        chunk = owner * per + per - 1

        @pl.when(owner != me)
        def _():
            home_in(chunk).wait_recv()

        late[owner] = back[chunk]
        return carry

    lax.fori_loop(0, groups, arrive, 0)

    def drain(chunk, carry):
        @pl.when(chunk // per != me)
        def _():
            forth_in(chunk).wait_send()
            home_in(chunk).wait_send()

        return carry

    lax.fori_loop(0, chunks, drain, 0)
    for step in range(1, groups):
        share(step).wait_send()

    @pl.when(seq < shards - 1)
    def _():
        def drain_chain(k, carry):
            chain(k).wait_send()
            return carry

        lax.fori_loop(0, per, drain_chain, 0)


def closing_kernel(groups, head_dim, part, late, grow, readout, o_hbm, ready, sem):
    chunks = part.shape[1] // CHUNK
    per = chunks // groups
    copies = []
    for chunk in range(chunks):
        columns = pl.ds(chunk * CHUNK, CHUNK)
        if chunk % per < per - 1:
            copies.append(
                pltpu.make_async_copy(part.at[:, columns], o_hbm.at[:, columns], sem.at[chunk])
            )
            copies[-1].start()
    for owner in range(groups):
        chunk = owner * per + per - 1
        columns = pl.ds(chunk * CHUNK, CHUNK)
        carried = mm(readout[...], right_side(late[owner]))
        growth = mm(grow[...], expander(chunk, 2 * LANES, CHUNK // head_dim, head_dim))
        ready[owner] = part[:, columns] + carried * growth
        copies.append(
            pltpu.make_async_copy(ready.at[owner], o_hbm.at[:, columns], sem.at[chunk])
        )
        copies[-1].start()
    for copy in copies:
        copy.wait()


def in_one(groups, shards, inputs, log_decay, input_map, output_map, skip_gain):
    tokens, width = inputs.shape
    state = input_map.shape[1]
    chunks = width // CHUNK
    per = chunks // groups
    head_dim = width // skip_gain.shape[0]
    vmem = pl.BlockSpec(memory_space=pltpu.VMEM)
    far = pl.BlockSpec(memory_space=pltpu.HBM)
    f32, bf16 = jnp.float32, jnp.bfloat16
    dma = pltpu.SemaphoreType.DMA
    parts = pl.pallas_call(
        functools.partial(whole_kernel, groups, shards, head_dim),
        out_shape=(
            jax.ShapeDtypeStruct((tokens, width), f32),
            jax.ShapeDtypeStruct((groups, state, CHUNK), f32),
            jax.ShapeDtypeStruct((tokens, 2 * LANES), bf16),
            jax.ShapeDtypeStruct((tokens, 3 * state), bf16),
        ),
        in_specs=[far] * 5,
        out_specs=[vmem] * 4,
        scratch_shapes=[
            pltpu.VMEM(log_decay.shape[::-1], f32),
            pltpu.VMEM(input_map.shape, f32),
            pltpu.VMEM(output_map.shape, f32),
            pltpu.VMEM((1, skip_gain.shape[0]), f32),
            pltpu.VMEM((chunks, tokens, CHUNK), f32),
            pltpu.VMEM((chunks, state, CHUNK), f32),
            pltpu.VMEM((chunks, state, CHUNK), f32),
            pltpu.VMEM((per, state, CHUNK), f32),
            pltpu.VMEM((per, state, CHUNK), f32),
            pltpu.VMEM((chunks, state, CHUNK), f32),
            pltpu.VMEM((state, 3 * BLOCK), bf16),
            pltpu.VMEM((state, 3 * BLOCK), bf16),
            pltpu.VMEM((2 * BLOCK, 3 * BLOCK), bf16),
            pltpu.VMEM((BLOCK, 3 * BLOCK), bf16),
            pltpu.VMEM((2 * BLOCK, 2 * LANES), bf16),
            pltpu.VMEM((3 * BLOCK, 2 * LANES), bf16),
            pltpu.VMEM((16, 3 * LANES), bf16),
            pltpu.VMEM((groups, 8, LANES), f32),
            dma((4,)),
            dma((chunks,)),
            dma((chunks,)),
            dma((chunks,)),
            dma((per,)),
            dma((per,)),
            dma((chunks,)),
            dma((chunks,)),
            dma((groups,)),
            dma((groups,)),
        ],
        compiler_params=pltpu.CompilerParams(
            collective_id=0, has_side_effects=True, vmem_limit_bytes=36 << 20
        ),
    )(
        *(
            pltpu.with_memory_space_constraint(operand, pltpu.HBM)
            for operand in (inputs, log_decay.T, input_map, output_map, skip_gain.reshape(1, -1))
        )
    )
    return pl.pallas_call(
        functools.partial(closing_kernel, groups, head_dim),
        out_shape=jax.ShapeDtypeStruct((tokens, width), f32),
        in_specs=[vmem] * 4,
        out_specs=pl.BlockSpec(memory_space=pl.ANY),
        scratch_shapes=[pltpu.VMEM((groups, tokens, CHUNK), f32), dma((chunks,))],
        compiler_params=pltpu.CompilerParams(vmem_limit_bytes=16 << 20),
    )(*parts)


def on_any(groups, shards, inputs, log_decay, input_map, output_map, skip_gain):
    tokens, width = inputs.shape
    heads = skip_gain.shape[0]
    head_dim = width // heads
    fits = (
        tokens == 2 * BLOCK
        and input_map.shape[1] == LANES
        and heads <= LANES
        and CHUNK % head_dim == 0
        and width % (groups * CHUNK) == 0
        and groups > 1
        and shards > 2
    )
    if fits:
        return in_one(groups, shards, inputs, log_decay, input_map, output_map, skip_gain)
    return on_device(inputs, log_decay, input_map, output_map, skip_gain)


def solution(mesh):
    in_specs = (
        P(("seq", "head"), None),
        P(("seq", "head"), None),
        P(("seq", "head"), None),
        P(("seq", "head"), None),
        P(),
    )
    out_specs = P(("seq", "head"), None)
    return jax.shard_map(
        functools.partial(on_any, mesh.shape["head"], mesh.shape["seq"]),
        mesh=mesh, in_specs=in_specs, out_specs=out_specs, check_vma=False,
    )
```

```python
import functools
import jax
import jax.numpy as jnp
from jax import lax
from jax.experimental import pallas as pl
from jax.experimental.pallas import tpu as pltpu
from jax.sharding import PartitionSpec as P

BLOCK = 128


PRECISE = lax.Precision.HIGHEST


def from_behind(value, axis, steps):
    count = lax.axis_size(axis)
    leading, last = (max(0, -steps), min(count, count - steps))
    return lax.ppermute(value, axis, [(source, source + steps) for source in range(leading, last)])


def scan_blocks(inputs, log_decay, input_map, output_map, head_dim):
    token_count = inputs.shape[0]
    width = inputs.shape[1]
    head_count = log_decay.shape[1]
    state_width = input_map.shape[1]
    blocks = token_count // BLOCK
    x_all = inputs.reshape(blocks, BLOCK, width)
    d_all = log_decay.reshape(blocks, BLOCK, head_count)
    b_all = input_map.reshape(blocks, BLOCK, state_width)
    c_all = output_map.reshape(blocks, BLOCK, state_width)
    running = jnp.cumsum(d_all, axis=1)
    run_heads = jnp.moveaxis(running, 2, 1)
    positions = jnp.arange(BLOCK)
    causal = positions[:, None] >= positions[None, :]
    spread = run_heads[:, :, :, None] - run_heads[:, :, None, :]
    decays = jnp.where(causal[None, None], jnp.exp(jnp.minimum(spread, 0.0)), 0.0)
    scores = jnp.einsum("bin,bjn->bij", c_all, b_all, precision=PRECISE)
    weighted = scores[:, None] * decays
    per_head = x_all.reshape(blocks, BLOCK, head_count, head_dim)
    within = jnp.einsum("bhij,bjhp->bihp", weighted, per_head, precision=PRECISE).reshape(
        blocks, BLOCK, width
    )
    closing = running[:, -1, :]
    remains = jnp.repeat(jnp.exp(closing[:, None, :] - running), head_dim, axis=2)
    own_state = jnp.einsum("bln,blw->bnw", b_all, x_all * remains, precision=PRECISE)
    totals = jnp.cumsum(closing, axis=0)
    before_total = totals - closing
    order = jnp.arange(blocks)
    earlier = order[:, None] > order[None, :]
    gap = before_total[:, None, :] - totals[None, :, :]
    link = jnp.where(earlier[:, :, None], jnp.exp(jnp.minimum(gap, 0.0)), 0.0)
    link_wide = jnp.repeat(link, head_dim, axis=2)
    entering = jnp.einsum("kjw,jnw->knw", link_wide, own_state, precision=PRECISE)
    final_weight = jnp.repeat(jnp.exp(totals[-1][None, :] - totals), head_dim, axis=1)
    memory = jnp.einsum("jw,jnw->nw", final_weight, own_state, precision=PRECISE)
    growth = jnp.repeat(jnp.exp(running), head_dim, axis=2)
    carried = jnp.einsum("bin,bnw->biw", c_all, entering, precision=PRECISE) * growth
    prefix = running + before_total[:, None, :]
    return (
        (within + carried).reshape(token_count, width),
        prefix.reshape(token_count, head_count),
        memory,
        totals[-1],
    )


def shard_chain(summed, memory, head_dim):
    factor = jnp.repeat(jnp.exp(summed), head_dim)[None, :]

    def advance(turn, incoming):
        return from_behind(factor * incoming + memory, "seq", 1)

    return lax.fori_loop(0, lax.axis_size("seq") - 1, advance, jnp.zeros_like(memory))


def on_device(inputs, log_decay, input_map, output_map, skip_gain):
    head_count = skip_gain.shape[0]
    head_dim = inputs.shape[1] // head_count
    state_width = input_map.shape[1]
    groups = lax.axis_size("head")
    local_heads = head_count // groups
    local_width = local_heads * head_dim
    results, prefix, memory, summed = scan_blocks(
        inputs, log_decay, input_map, output_map, head_dim
    )
    got_sum, got_state = (
        lax.all_to_all(
            summed.reshape(1, groups, local_heads), "head", split_axis=1, concat_axis=1, tiled=True
        ),
        lax.all_to_all(
            memory.reshape(state_width, groups, local_width),
            "head",
            split_axis=1,
            concat_axis=1,
            tiled=True,
        ),
    )

    def within_shard(carry, item):
        total_decay, total_state = carry
        decay_here, state_here = item
        scale_now = jnp.repeat(jnp.exp(decay_here), head_dim)[None, :]
        return ((total_decay + decay_here, scale_now * total_state + state_here), carry)

    start_carry = (
        jnp.zeros((local_heads,), jnp.float32),
        jnp.zeros((state_width, local_width), jnp.float32),
    )
    (shard_decay, shard_state), (before_decay, before_state) = lax.scan(
        within_shard, start_carry, (got_sum[0], jnp.moveaxis(got_state, 1, 0))
    )
    incoming = shard_chain(shard_decay, shard_state, head_dim)
    per_source = (
        jnp.repeat(jnp.exp(before_decay), head_dim, axis=1)[:, None, :] * incoming[None]
        + before_state
    )
    back = lax.all_to_all(
        jnp.moveaxis(per_source, 0, 1), "head", split_axis=1, concat_axis=1, tiled=True
    )
    arrived = back.reshape(state_width, head_count * head_dim)
    returned = results + jnp.dot(output_map, arrived, precision=PRECISE) * jnp.repeat(
        jnp.exp(prefix), head_dim, axis=1
    )
    return returned + inputs * jnp.repeat(skip_gain, head_dim)[None, :]


MESH = pl.DeviceIdType.MESH
CHUNK = 256
LANES = 128


def two(value):
    high = value.astype(jnp.bfloat16)
    return high, (value - high.astype(jnp.float32)).astype(jnp.bfloat16)


def three(value):
    high = value.astype(jnp.bfloat16)
    rest = value - high.astype(jnp.float32)
    middle = rest.astype(jnp.bfloat16)
    return high, middle, (rest - middle.astype(jnp.float32)).astype(jnp.bfloat16)


def left_side(value):
    high, low = two(value)
    return jnp.concatenate([high, high, low], axis=1)


def right_side(value):
    high, low = two(value)
    return jnp.concatenate([high, low, high], axis=0)


def mm(a, b):
    return jnp.dot(a, b, preferred_element_type=jnp.float32)


def full_mm(a, b, dims):
    return lax.dot_general(
        a, b, (dims, ((), ())), precision=PRECISE, preferred_element_type=jnp.float32
    )


def expander(chunk, depth, heads_per_chunk, head_dim):
    row = lax.broadcasted_iota(jnp.int32, (depth, CHUNK), 0) & (LANES - 1)
    column = lax.broadcasted_iota(jnp.int32, (depth, CHUNK), 1) // head_dim
    hit = row == column + chunk * heads_per_chunk
    return jnp.where(hit, 1.0, 0.0).astype(jnp.bfloat16)


def whole_kernel(
    groups, shards, head_dim,
    x_hbm, d_hbm, b_hbm, c_hbm, g_hbm, o_ref, late, grow, readout,
    d_ref, b_ref, c_ref, g_ref, xbuf, mbuf, rbuf, sbuf, sout, back,
    state1, state2, first, second, lift, spread, rows, loss,
    isem, xsem, fsend, frecv, csend, crecv, bsend, brecv, lsend, lrecv,
):
    seq = lax.axis_index("seq")
    me = lax.axis_index("head")
    chunks = xbuf.shape[0]
    per = chunks // groups
    state = b_ref.shape[1]
    hpc = CHUNK // head_dim

    def x_copy(chunk):
        columns = pl.ds(pl.multiple_of(chunk * CHUNK, CHUNK), CHUNK)
        return pltpu.make_async_copy(x_hbm.at[:, columns], xbuf.at[chunk], xsem.at[chunk])

    def columns_of(chunk):
        return pl.ds(pl.multiple_of(chunk * CHUNK, CHUNK), CHUNK)

    def share(step):
        return pltpu.make_async_remote_copy(
            src_ref=loss.at[me],
            dst_ref=loss.at[me],
            send_sem=lsend.at[step],
            recv_sem=lrecv.at[me],
            device_id={"head": (me + step) % groups},
            device_id_type=MESH,
        )

    def share_in(source):
        return pltpu.make_async_remote_copy(
            src_ref=loss.at[source],
            dst_ref=loss.at[source],
            send_sem=lsend.at[0],
            recv_sem=lrecv.at[source],
            device_id={"head": (me + 1) % groups},
            device_id_type=MESH,
        )

    def at_turn(turn):
        k = turn // groups
        owner = (me + 1 + turn % groups) % groups
        return k, owner, owner * per + k

    def forth(chunk, k, owner):
        return pltpu.make_async_remote_copy(
            src_ref=mbuf.at[chunk],
            dst_ref=rbuf.at[me * per + k],
            send_sem=fsend.at[chunk],
            recv_sem=frecv.at[me * per + k],
            device_id={"head": owner},
            device_id_type=MESH,
        )

    def forth_in(slot):
        return pltpu.make_async_remote_copy(
            src_ref=mbuf.at[slot],
            dst_ref=rbuf.at[slot],
            send_sem=fsend.at[slot],
            recv_sem=frecv.at[slot],
            device_id={"head": (me + 1) % groups},
            device_id_type=MESH,
        )

    def chain(k):
        return pltpu.make_async_remote_copy(
            src_ref=sout.at[k],
            dst_ref=sbuf.at[k],
            send_sem=csend.at[k],
            recv_sem=crecv.at[k],
            device_id={"seq": (seq + 1) % shards},
            device_id_type=MESH,
        )

    def home(slot, k, target):
        return pltpu.make_async_remote_copy(
            src_ref=rbuf.at[slot],
            dst_ref=back.at[me * per + k],
            send_sem=bsend.at[slot],
            recv_sem=brecv.at[me * per + k],
            device_id={"head": target},
            device_id_type=MESH,
        )

    def home_in(slot):
        return pltpu.make_async_remote_copy(
            src_ref=rbuf.at[slot],
            dst_ref=back.at[slot],
            send_sem=bsend.at[slot],
            recv_sem=brecv.at[slot],
            device_id={"head": (me + 1) % groups},
            device_id_type=MESH,
        )

    def load(turn, carry):
        x_copy(at_turn(turn)[2]).start()
        return carry

    barrier = pltpu.get_barrier_semaphore()
    for step in range(1, groups):
        pl.semaphore_signal(
            barrier, inc=1, device_id={"head": (me + step) % groups}, device_id_type=MESH
        )

    @pl.when(seq > 0)
    def _():
        pl.semaphore_signal(
            barrier, inc=1, device_id={"seq": (seq + shards - 1) % shards}, device_id_type=MESH
        )

    pairs = ((d_hbm, d_ref), (b_hbm, b_ref), (g_hbm, g_ref), (c_hbm, c_ref))
    small = [pltpu.make_async_copy(*pair, isem.at[i]) for i, pair in enumerate(pairs)]
    small[0].start()
    small[1].start()
    small[2].start()
    lax.fori_loop(0, chunks, load, 0)
    small[3].start()

    heads = d_ref.shape[0]
    below = lax.broadcasted_iota(jnp.int32, (BLOCK, BLOCK), 0)
    above = lax.broadcasted_iota(jnp.int32, (BLOCK, BLOCK), 1)
    causal = below >= above
    ones = jnp.where(causal, 1.0, 0.0).astype(jnp.bfloat16)
    small[0].wait()
    padding = jnp.zeros((LANES - heads, d_ref.shape[1]), jnp.float32)
    decay = jnp.concatenate([d_ref[...], padding], axis=0).T
    run1 = sum(mm(ones, part) for part in three(decay[:BLOCK]))
    run2 = sum(mm(ones, part) for part in three(decay[BLOCK:]))
    end1, end2 = run1[BLOCK - 1 :], run2[BLOCK - 1 :]
    mid1, mid2 = run1[BLOCK // 2 - 1 : BLOCK // 2], run2[BLOCK // 2 - 1 : BLOCK // 2]
    total = end1 + end2
    up = jnp.concatenate([jnp.exp(mid1 - run1), jnp.exp(mid2 - run2)], axis=0)
    lift[...] = jnp.concatenate(two(up), axis=1)
    small[2].wait()
    gain = jnp.concatenate([g_ref[...], jnp.zeros((1, LANES - heads), jnp.float32)], axis=1)
    line = lax.broadcasted_iota(jnp.int32, (16, LANES), 0)
    picked = jnp.where(line == 1, jnp.exp(total - mid1), 0.0)
    picked = jnp.where(line == 2, jnp.exp(end2 - mid2), picked)
    picked = jnp.where(line == 3, gain, picked)
    rows[...] = jnp.concatenate(three(picked), axis=1)
    loss[me] = jnp.broadcast_to(jnp.exp(total), (8, LANES))
    small[1].wait()
    b1, b2 = b_ref[:BLOCK], b_ref[BLOCK:]
    state1[...] = left_side(b1.T)
    state2[...] = left_side(b2.T)

    @pl.when(seq == 0)
    def _():
        sbuf[...] = jnp.zeros_like(sbuf)

    pl.semaphore_wait(barrier, groups - 1 + jnp.minimum(shards - 1 - seq, 1))
    for step in range(1, groups):
        share(step).start()

    def weighed(chunk):
        scale = mm(lift[...], expander(chunk, 2 * LANES, hpc, head_dim))
        value = xbuf[chunk] * scale
        return right_side(value[:BLOCK]), right_side(value[BLOCK:])

    def send(turn, carry):
        k, owner, chunk = at_turn(turn)
        x_copy(chunk).wait()
        w1, w2 = weighed(chunk)
        lines = mm(rows[...], expander(chunk, 3 * LANES, hpc, head_dim))
        memory = mm(state1[...], w1) * lines[1:2] + mm(state2[...], w2) * lines[2:3]

        @pl.when(owner == me)
        def _():
            rbuf[chunk] = memory

        @pl.when(owner != me)
        def _():
            mbuf[chunk] = memory
            forth(chunk, k, owner).start()

        return carry

    lax.fori_loop(0, chunks, send, 0)

    down = jnp.concatenate(
        [
            jnp.exp(run1 - mid1),
            jnp.exp(run2 - mid2),
            jnp.exp(run2 + (end1 - mid1)),
        ],
        axis=0,
    )
    spread[...] = jnp.concatenate(two(down), axis=1)
    grow[...] = jnp.concatenate(
        two(jnp.concatenate([jnp.exp(run1), jnp.exp(run2 + end1)], axis=0)), axis=1
    )
    small[3].wait()
    c1, c2 = c_ref[:BLOCK], c_ref[BLOCK:]
    last = ((1,), (1,))
    own1 = jnp.where(causal, full_mm(c1, b1, last), 0.0)
    own2 = jnp.where(causal, full_mm(c2, b2, last), 0.0)
    cross = full_mm(c2, b1, last)
    first[...] = left_side(jnp.concatenate([own1, cross], axis=0))
    second[...] = left_side(own2)
    readout[...] = left_side(c_ref[...])

    def local(turn, carry):
        k, owner, chunk = at_turn(turn)
        w1, w2 = weighed(chunk)
        scale = mm(spread[...], expander(chunk, 2 * LANES, hpc, head_dim))
        lines = mm(rows[...], expander(chunk, 3 * LANES, hpc, head_dim))
        y1 = mm(first[...], w1)
        y2 = mm(second[...], w2)
        columns = columns_of(chunk)
        o_ref[:BLOCK, columns] = y1[:BLOCK] * scale[:BLOCK] + lines[3:4] * xbuf[chunk, :BLOCK]
        o_ref[BLOCK:, columns] = (
            y2 * scale[BLOCK : 2 * BLOCK]
            + y1[BLOCK:] * scale[2 * BLOCK :]
            + lines[3:4] * xbuf[chunk, BLOCK:]
        )
        return carry

    lax.fori_loop(0, groups, local, 0)
    for step in range(1, groups):
        share_in((me + step) % groups).wait_recv()
    tall = -(-groups // 16) * 16
    line = lax.broadcasted_iota(jnp.int32, (tall, LANES), 0)
    losses = jnp.zeros((tall, LANES), jnp.float32)
    for j in range(groups):
        losses = jnp.where(line == j, loss[j, :1], losses)
    losses = jnp.concatenate(three(losses), axis=1)

    def link(k, carry):
        lax.fori_loop(
            jnp.minimum((k + 1) * groups, chunks), jnp.minimum((k + 2) * groups, chunks), local, 0
        )
        for step in range(1, groups):
            forth_in(((me + step) % groups) * per + k).wait_recv()
        wide = mm(losses, expander(me * per + k, 3 * LANES, hpc, head_dim))
        factors = [wide[j : j + 1] for j in range(groups)]
        shard = rbuf[k]
        shard_factor = factors[0]
        for j in range(1, groups):
            shard = factors[j] * shard + rbuf[j * per + k]
            shard_factor = shard_factor * factors[j]
        sout[k] = shard

        @pl.when(seq > 0)
        def _():
            chain(k).wait_recv()

        @pl.when(seq < shards - 1)
        def _():
            sout[k] = shard_factor * sbuf[k] + sout[k]
            chain(k).start()

        incoming = sbuf[k]
        for j in range(groups):
            slot = j * per + k
            here = rbuf[slot]
            rbuf[slot] = incoming

            @pl.when(me == j)
            def _():
                back[slot] = incoming

            @pl.when(me != j)
            def _():
                home(slot, k, j).start()

            incoming = factors[j] * incoming + here
        return carry

    lax.fori_loop(0, per, link, 0)

    def finish(turn, carry):
        k = turn // groups
        owner = (me + turn % groups) % groups
        chunk = owner * per + k

        @pl.when(owner != me)
        def _():
            home_in(chunk).wait_recv()

        carried = mm(readout[...], right_side(back[chunk]))
        growth = mm(grow[...], expander(chunk, 2 * LANES, hpc, head_dim))
        columns = columns_of(chunk)
        o_ref[:, columns] = o_ref[:, columns] + carried * growth
        return carry

    lax.fori_loop(0, chunks - groups, finish, 0)

    def arrive(turn, carry):
        owner = (me + turn) % groups
        chunk = owner * per + per - 1

        @pl.when(owner != me)
        def _():
            home_in(chunk).wait_recv()

        late[owner] = back[chunk]
        return carry

    lax.fori_loop(0, groups, arrive, 0)

    def drain(chunk, carry):
        @pl.when(chunk // per != me)
        def _():
            forth_in(chunk).wait_send()
            home_in(chunk).wait_send()

        return carry

    lax.fori_loop(0, chunks, drain, 0)
    for step in range(1, groups):
        share(step).wait_send()

    @pl.when(seq < shards - 1)
    def _():
        def drain_chain(k, carry):
            chain(k).wait_send()
            return carry

        lax.fori_loop(0, per, drain_chain, 0)


def closing_kernel(groups, head_dim, part, late, grow, readout, o_hbm, ready, sem):
    chunks = part.shape[1] // CHUNK
    per = chunks // groups
    copies = []
    half = part.shape[0] // 2
    for piece in range(2 * groups if per > 1 else 0):
        columns = pl.ds(piece // 2 * per * CHUNK, (per - 1) * CHUNK)
        where = (pl.ds(piece % 2 * half, half), columns)
        copies.append(
            pltpu.make_async_copy(part.at[where], o_hbm.at[where], sem.at[groups + piece])
        )
        copies[-1].start()
    for owner in range(groups):
        chunk = owner * per + per - 1
        columns = pl.ds(chunk * CHUNK, CHUNK)
        carried = mm(readout[...], right_side(late[owner]))
        growth = mm(grow[...], expander(chunk, 2 * LANES, CHUNK // head_dim, head_dim))
        ready[owner] = part[:, columns] + carried * growth
        copies.append(
            pltpu.make_async_copy(ready.at[owner], o_hbm.at[:, columns], sem.at[owner])
        )
        copies[-1].start()
    for copy in copies:
        copy.wait()


def in_one(groups, shards, inputs, log_decay, input_map, output_map, skip_gain):
    tokens, width = inputs.shape
    state = input_map.shape[1]
    chunks = width // CHUNK
    per = chunks // groups
    head_dim = width // skip_gain.shape[0]
    vmem = pl.BlockSpec(memory_space=pltpu.VMEM)
    far = pl.BlockSpec(memory_space=pltpu.HBM)
    f32, bf16 = jnp.float32, jnp.bfloat16
    dma = pltpu.SemaphoreType.DMA
    parts = pl.pallas_call(
        functools.partial(whole_kernel, groups, shards, head_dim),
        out_shape=(
            jax.ShapeDtypeStruct((tokens, width), f32),
            jax.ShapeDtypeStruct((groups, state, CHUNK), f32),
            jax.ShapeDtypeStruct((tokens, 2 * LANES), bf16),
            jax.ShapeDtypeStruct((tokens, 3 * state), bf16),
        ),
        in_specs=[far] * 5,
        out_specs=[vmem] * 4,
        scratch_shapes=[
            pltpu.VMEM(log_decay.shape[::-1], f32),
            pltpu.VMEM(input_map.shape, f32),
            pltpu.VMEM(output_map.shape, f32),
            pltpu.VMEM((1, skip_gain.shape[0]), f32),
            pltpu.VMEM((chunks, tokens, CHUNK), f32),
            pltpu.VMEM((chunks, state, CHUNK), f32),
            pltpu.VMEM((chunks, state, CHUNK), f32),
            pltpu.VMEM((per, state, CHUNK), f32),
            pltpu.VMEM((per, state, CHUNK), f32),
            pltpu.VMEM((chunks, state, CHUNK), f32),
            pltpu.VMEM((state, 3 * BLOCK), bf16),
            pltpu.VMEM((state, 3 * BLOCK), bf16),
            pltpu.VMEM((2 * BLOCK, 3 * BLOCK), bf16),
            pltpu.VMEM((BLOCK, 3 * BLOCK), bf16),
            pltpu.VMEM((2 * BLOCK, 2 * LANES), bf16),
            pltpu.VMEM((3 * BLOCK, 2 * LANES), bf16),
            pltpu.VMEM((16, 3 * LANES), bf16),
            pltpu.VMEM((groups, 8, LANES), f32),
            dma((4,)),
            dma((chunks,)),
            dma((chunks,)),
            dma((chunks,)),
            dma((per,)),
            dma((per,)),
            dma((chunks,)),
            dma((chunks,)),
            dma((groups,)),
            dma((groups,)),
        ],
        compiler_params=pltpu.CompilerParams(
            collective_id=0, has_side_effects=True, vmem_limit_bytes=36 << 20
        ),
    )(
        *(
            pltpu.with_memory_space_constraint(operand, pltpu.HBM)
            for operand in (inputs, log_decay.T, input_map, output_map, skip_gain.reshape(1, -1))
        )
    )
    return pl.pallas_call(
        functools.partial(closing_kernel, groups, head_dim),
        out_shape=jax.ShapeDtypeStruct((tokens, width), f32),
        in_specs=[vmem] * 4,
        out_specs=pl.BlockSpec(memory_space=pl.ANY),
        scratch_shapes=[pltpu.VMEM((groups, tokens, CHUNK), f32), dma((3 * groups,))],
        compiler_params=pltpu.CompilerParams(vmem_limit_bytes=16 << 20),
    )(*parts)


def on_any(groups, shards, inputs, log_decay, input_map, output_map, skip_gain):
    tokens, width = inputs.shape
    heads = skip_gain.shape[0]
    head_dim = width // heads
    fits = (
        tokens == 2 * BLOCK
        and input_map.shape[1] == LANES
        and heads <= LANES
        and CHUNK % head_dim == 0
        and width % (groups * CHUNK) == 0
        and groups > 1
        and shards > 2
    )
    if fits:
        return in_one(groups, shards, inputs, log_decay, input_map, output_map, skip_gain)
    return on_device(inputs, log_decay, input_map, output_map, skip_gain)


def solution(mesh):
    in_specs = (
        P(("seq", "head"), None),
        P(("seq", "head"), None),
        P(("seq", "head"), None),
        P(("seq", "head"), None),
        P(),
    )
    out_specs = P(("seq", "head"), None)
    return jax.shard_map(
        functools.partial(on_any, mesh.shape["head"], mesh.shape["seq"]),
        mesh=mesh, in_specs=in_specs, out_specs=out_specs, check_vma=False,
    )
```
